256 devices in a mesh: mem: 8 (over x_lo, y), tile: 32 (over z, x_hi, core).
Axes of the slice: x: 4 (x_hi: 2, x_lo: 2; x = x_hi * 2 + x_lo), y: 4, z: 8, core: 2. Of those that a mesh axis runs over, the one named last changes fastest.
Arguments:
- perturbations: bfloat16 [3, 256, 512, 256], P(None, 'mem', 'tile'), may hold values from -0.375 to 0.375
- control: float32 [256, 512, 256], P('mem', 'tile'), may hold values from -15 to 15
- innovation: float32 [3, 512, 256], P(None, 'tile'), may hold values from -6 to 6
- obs_weight: float32 [3, 512, 256], P(None, 'tile'), may hold values from 2 to 32
- diffusion: float32 [512, 256], P('tile'), may hold values from 0.04 to 0.18
- advection: float32 [512, 256], P('tile'), may hold values from 0.08 to 0.3
- upwind: int32 [512, 256], P('tile'), may hold values from 0 to 1
Outputs:
- gradient: float32 [256, 512, 256], P('mem', 'tile')
- hessian_product: float32 [256, 512, 256], P('mem', 'tile')
- step_length: float32 [], replicated
The draws below stay inside these ranges and needn't reach their ends.
All inputs are finite; a program needn't handle non-finite values.
Results may differ from the reference program's by a relative error of at most 0.0003.
Values sent between devices are 32-bit elements; how exact they have to be, the bound alone decides.
A program may use at most 64 MiB of HBM per device.

```python
import math
import jax
import jax.numpy as jnp
from jax import lax

M = 256
NT = 3
SWEEPS = 4
NY = 256
NX = 512


def draw_control(key, part):
    member_pos = jnp.arange(M, dtype=jnp.float32)[:, None, None] / M
    row_pos = jnp.arange(NX, dtype=jnp.float32)[None, :, None] / NX
    base = jax.random.truncated_normal(key, -5.0, 5.0, (M, NX, NY), jnp.float32)
    scale = jnp.sqrt((1.0 + 2.0 * member_pos) * (1.0 + 2.0 * row_pos))
    return (base * scale).astype(jnp.float32)


def plant(entries, stream_key, least, high):
    dims = entries.shape
    place = [jax.random.randint(jax.random.fold_in(stream_key, axis), (), 0, dims[axis]) for axis in range(len(dims))]
    entries = entries.at[tuple(place)].set(least)
    longest = dims.index(max(dims))
    place[longest] = (place[longest] + 1) % dims[longest]
    return entries.at[tuple(place)].set(high)


def block_levels(stream_key, extent, cuts, least, high):
    level = 1.0
    for axis_at, parts in cuts:
        heights = jax.random.uniform(jax.random.fold_in(jax.random.fold_in(stream_key, 6), axis_at), (parts,), jnp.float32, least / len(cuts), high / len(cuts))
        level = level * jnp.repeat(jnp.exp(heights), extent[axis_at] // parts).reshape((-1,) + (1,) * (len(extent) - 1 - axis_at))
    return level


def gaussian(stream_key, dims, width, most, split=(), kind=jnp.bfloat16):
    result = jax.random.normal(stream_key, dims, jnp.float32) * width
    if len(split) > 0:
        result = block_levels(stream_key, dims, split, -0.22, 0.18) * result
    return jnp.clip(result, min=-most, max=most).astype(kind)


def setup_inputs(seed: int = 0) -> dict:
    streams_of = jax.random.split(jax.random.key(seed), 8)
    return {
        "perturbations": gaussian(streams_of[0], (NT, M, NX, NY), M ** -0.5, 0.375, ((1, 8), (2, 32))),
        "control": draw_control(jax.random.fold_in(streams_of[7], 71), 0),
        "innovation": gaussian(streams_of[2], (NT, NX, NY), 1.0, 6.0, ((1, 32),), jnp.float32),
        "obs_weight": jnp.clip(jnp.exp(math.log(32.0) - 2.7725887 * jax.random.uniform(streams_of[3], (NT, NX, NY), jnp.float32) ** block_levels(streams_of[3], (NT, NX, NY), ((1, 32),), -0.2, 0.2)), 2.0, 32.0),
        "diffusion": jnp.clip(0.04 + 0.14000001 * jax.random.uniform(streams_of[4], (NX, NY), jnp.float32) ** block_levels(streams_of[4], (NX, NY), ((0, 32),), -0.2, 0.2), 0.04, 0.18),
        "advection": jnp.clip(0.08 + 0.22000001 * jax.random.uniform(streams_of[5], (NX, NY), jnp.float32) ** block_levels(streams_of[5], (NX, NY), ((0, 32),), -0.2, 0.2), 0.08, 0.3),
        "upwind": plant(jax.random.randint(streams_of[6], (NX, NY), 0, 2), jax.random.fold_in(streams_of[6], 1), 0, 1).astype(jnp.int32),
    }


member_block = 8


def pad_cells(values):
    widths = [(0, 0)] * (values.ndim - 2) + [(1, 1), (1, 1)]
    return jnp.pad(values, widths)


def forward_sweep(values, kappa_field, advect_field, upwind_field):
    padded = pad_cells(values)
    below = padded[..., 2:, 1:-1]
    above = padded[..., :-2, 1:-1]
    spread = below + above + padded[..., 1:-1, 2:] + padded[..., 1:-1, :-2] - 4.0 * values
    upwind_value = jnp.where(upwind_field == 1, below, above)
    return values + kappa_field * spread - advect_field * (values - upwind_value)


def adjoint_sweep(values, kappa_field, advect_field, upwind_field):
    weighted = kappa_field * values
    carried = advect_field * values
    to_lower = jnp.where(upwind_field == 0, carried, 0.0)
    to_upper = jnp.where(upwind_field == 1, carried, 0.0)
    padded = pad_cells(weighted)
    spread = padded[..., 2:, 1:-1] + padded[..., :-2, 1:-1] + padded[..., 1:-1, 2:] + padded[..., 1:-1, :-2] - 4.0 * weighted
    returned = pad_cells(to_lower)[..., 2:, 1:-1] + pad_cells(to_upper)[..., :-2, 1:-1]
    return values + spread - carried + returned


def reference(perturbations, control, innovation, obs_weight, diffusion, advection, upwind):
    groups = M // member_block
    pert_groups = jnp.moveaxis(perturbations.reshape(NT, groups, member_block, NX, NY), 1, 0)
    ctrl_groups = control.reshape(groups, member_block, NX, NY)

    def localise(values):
        for repeat in range(SWEEPS):
            values = forward_sweep(values, diffusion, advection, upwind)
        return values

    def localise_adjoint(values):
        for repeat in range(SWEEPS):
            values = adjoint_sweep(values, diffusion, advection, upwind)
        return values

    def project(field_groups):
        def one_group(inputs_pair):
            members, pert_block = inputs_pair
            spread_out = localise(members)
            return jnp.sum(pert_block.astype(jnp.float32) * spread_out[None], axis=1)
        return jnp.sum(lax.map(one_group, (field_groups, pert_groups)), axis=0)

    def adjoint(field_groups, weights_time):
        def one_group(inputs_pair):
            members, pert_block = inputs_pair
            pulled = jnp.sum(pert_block.astype(jnp.float32) * weights_time[:, None], axis=0)
            return members + localise_adjoint(pulled)
        return lax.map(one_group, (field_groups, pert_groups))

    increment = project(ctrl_groups)
    misfit = obs_weight * (increment - innovation)
    grad_groups = adjoint(ctrl_groups, misfit)
    image = project(grad_groups)
    weighted_image = obs_weight * image
    hess_groups = adjoint(grad_groups, weighted_image)
    gradient = grad_groups.reshape(M, NX, NY)
    hessian_product = hess_groups.reshape(M, NX, NY)
    squares = jnp.sum(gradient * gradient)
    curvature = squares + jnp.sum(image * weighted_image)
    return gradient, hessian_product, squares / curvature
```

```python
import functools

import jax
import jax.numpy as jnp
from jax import lax
from jax.experimental import pallas as pl
from jax.experimental.pallas import tpu as pltpu
from jax.sharding import PartitionSpec as P

MESH = pl.DeviceIdType.MESH
SUB = 8
LANES = 128
HALVES = 2
NT = 3
ROWS = 16
MEMBERS = 32
GROUPS = MEMBERS // SUB
MEM_COUNT = 8
TILE_COUNT = 32
WIDE = 8
EXT = ROWS + 2 * WIDE
NEAR = 4
FORWARD = 0
ADJOINT = 5


def kernel(
    ctrl,
    pert,
    innov,
    weight,
    diff,
    adv,
    upw,
    grad_out,
    hess_out,
    step_out,
    ctrl_nat,
    pert_half,
    pert_nat,
    pert_t,
    small_in,
    upw_in,
    obs_in,
    raw,
    coef,
    field,
    ping,
    pong,
    pulled,
    grad,
    pulled_2,
    edge_1,
    mid_1,
    edge_2,
    mid_2,
    mis,
    scal,
    grad_nat,
    hess_nat,
    in_sem,
    out_sem,
    halo_send,
    halo_recv,
    red_send,
    red_recv,
    scal_send,
    scal_recv,
):
    t = lax.axis_index("tile")
    m = lax.axis_index("mem")
    nxt = lax.rem(t + 1, TILE_COUNT)
    prv = lax.rem(t + TILE_COUNT - 1, TILE_COUNT)

    barrier = pltpu.get_barrier_semaphore()

    def greet_tile(k, c):
        pl.semaphore_signal(
            barrier, inc=1, device_id=(m, lax.rem(t + k, TILE_COUNT)), device_id_type=MESH
        )
        return c

    lax.fori_loop(1, TILE_COUNT, greet_tile, 0)
    for k in range(1, MEM_COUNT):
        pl.semaphore_signal(
            barrier, inc=1, device_id=(lax.rem(m + k, MEM_COUNT), t), device_id_type=MESH
        )

    loads = []
    for h in range(HALVES):
        cols = pl.ds(h * LANES, LANES)
        loads.append((ctrl.at[:, cols], ctrl_nat.at[h]))
        loads.append((diff.at[:, cols], small_in.at[0, h]))
        loads.append((adv.at[:, cols], small_in.at[1, h]))
        loads.append((upw.at[:, cols], upw_in.at[h]))
        loads.append((innov.at[:, cols], obs_in.at[0, h]))
        loads.append((weight.at[:, cols], obs_in.at[1, h]))
    loads.append((pert, pert_half))
    loads = [
        pltpu.make_async_copy(src, dst, in_sem.at[n]) for n, (src, dst) in enumerate(loads)
    ]
    for copy in loads:
        copy.start()

    lane = lax.broadcasted_iota(jnp.int32, (SUB, LANES), 1)
    low_sub = lax.broadcasted_iota(jnp.int32, (SUB, LANES), 0) < SUB // 2
    at_last = lane == LANES - 1
    at_first = lane == 0

    for copy in loads[:-1]:
        copy.wait()

    def place_control(r, c):
        for h in range(HALVES):
            for g in range(GROUPS):
                field[r + NEAR, h, pl.ds(SUB * g, SUB), :] = ctrl_nat[
                    h, pl.ds(SUB * g * ROWS + r, SUB, stride=ROWS), :
                ]
        return c

    lax.fori_loop(0, ROWS, place_control, 0, unroll=2)
    for h in range(HALVES):
        raw[0, h, pl.ds(WIDE, ROWS), :] = small_in[0, h]
        raw[1, h, pl.ds(WIDE, ROWS), :] = small_in[1, h]
        raw[2, h, pl.ds(WIDE, ROWS), :] = jnp.where(upw_in[h] == 1, 1.0, 0.0)

    def to_neighbours(buffer, own, depth, first):
        copies = []
        for n, (src_row, dst_row, dest) in enumerate(
            ((own, own + ROWS, prv), (own + ROWS - depth, own - depth, nxt))
        ):
            copies.append(
                pltpu.make_async_remote_copy(
                    src_ref=buffer(src_row, depth),
                    dst_ref=buffer(dst_row, depth),
                    send_sem=halo_send.at[first + n],
                    recv_sem=halo_recv.at[first + n],
                    device_id=(m, dest),
                    device_id_type=MESH,
                )
            )
        for copy in copies:
            copy.start()
        return copies

    def rows_of(ref):
        return lambda start, count: ref.at[pl.ds(start, count)]

    pl.semaphore_wait(barrier, TILE_COUNT - 1 + MEM_COUNT - 1)

    coef_copies = to_neighbours(
        lambda start, count: raw.at[:, :, pl.ds(start, count), :], WIDE, WIDE, 0
    )
    ctrl_copies = to_neighbours(rows_of(field), NEAR, NEAR, 2)

    loads[-1].wait()

    def widen(q, c):
        rows = pl.ds(pl.multiple_of(q * ROWS, ROWS), ROWS)
        for h in range(HALVES):
            pert_nat[h, rows, :] = pert_half[rows, pl.ds(h * LANES, LANES)].astype(jnp.float32)
        return c

    lax.fori_loop(0, NT * MEMBERS, widen, 0, unroll=4)

    def place_pert(r, c):
        for n in range(NT):
            for h in range(HALVES):
                for g in range(GROUPS):
                    pert_t[n, r, h, pl.ds(SUB * g, SUB), :] = pert_nat[
                        h, pl.ds((n * MEMBERS + SUB * g) * ROWS + r, SUB, stride=ROWS), :
                    ]
        return c

    lax.fori_loop(0, ROWS, place_pert, 0)

    for copy in coef_copies:
        copy.wait()

    row = lax.broadcasted_iota(jnp.int32, (EXT, LANES), 0)
    col = lax.broadcasted_iota(jnp.int32, (EXT, LANES), 1)
    top = jnp.logical_and(row == WIDE, t == 0)
    bottom = jnp.logical_and(row == WIDE + ROWS - 1, t == TILE_COUNT - 1)
    kappa = [raw[0, h] for h in range(HALVES)]
    right = [pltpu.roll(k, LANES - 1, 1) for k in kappa]
    left = [pltpu.roll(k, 1, 1) for k in kappa]
    right = [jnp.where(col == LANES - 1, right[1], right[0]), jnp.where(col == LANES - 1, 0.0, right[1])]
    left = [jnp.where(col == 0, 0.0, left[0]), jnp.where(col == 0, left[0], left[1])]
    for h in range(HALVES):
        k = kappa[h]
        a = raw[1, h]
        u = raw[2, h]
        centre = 1.0 - 4.0 * k - a
        below = k + a * u
        above = k + a * (1.0 - u)
        edge_right = jnp.logical_and(col == LANES - 1, h == HALVES - 1)
        edge_left = jnp.logical_and(col == 0, h == 0)
        coef[FORWARD + 0, h] = centre
        coef[FORWARD + 1, h] = jnp.where(bottom, 0.0, below)
        coef[FORWARD + 2, h] = jnp.where(top, 0.0, above)
        coef[FORWARD + 3, h] = jnp.where(edge_right, 0.0, k)
        coef[FORWARD + 4, h] = jnp.where(edge_left, 0.0, k)
        coef[ADJOINT + 0, h] = centre
        coef[ADJOINT + 1, h] = jnp.where(bottom, 0.0, pltpu.roll(above, EXT - 1, 0))
        coef[ADJOINT + 2, h] = jnp.where(top, 0.0, pltpu.roll(below, 1, 0))
        coef[ADJOINT + 3, h] = right[h]
        coef[ADJOINT + 4, h] = left[h]

    def sweep(src, src_own, dst, dst_own, kind, first, last, add=None, add_own=0):
        def two_rows(i, c):
            r = first + 2 * i
            factor = [
                [
                    [
                        coef[kind + n, h, pl.ds(r + d + WIDE, SUB, stride=0), :]
                        for h in range(HALVES)
                    ]
                    for n in range(5)
                ]
                for d in range(2)
            ]
            for g in range(GROUPS):
                part = pl.ds(SUB * g, SUB)
                lines = [
                    [src[r + src_own + d, h, part, :] for h in range(HALVES)]
                    for d in range(-1, 3)
                ]
                for d in range(2):
                    above, centre, below = lines[d], lines[d + 1], lines[d + 2]
                    right = [pltpu.roll(x, LANES - 1, 1) for x in centre]
                    left = [pltpu.roll(x, 1, 1) for x in centre]
                    right = [jnp.where(at_last, right[1], right[0]), right[1]]
                    left = [left[0], jnp.where(at_first, left[0], left[1])]
                    for h in range(HALVES):
                        f = [factor[d][n][h] for n in range(5)]
                        value = (f[0] * centre[h] + f[1] * below[h]) + (
                            f[2] * above[h] + (f[3] * right[h] + f[4] * left[h])
                        )
                        if add is not None:
                            value = value + add[r + d + add_own, h, part, :]
                        dst[r + d + dst_own, h, part, :] = value
            return c

        lax.fori_loop(0, (last - first) // 2, two_rows, 0)

    def four_sweeps(src, src_own, dst, dst_own, kind, margin, add=None, add_own=0):
        steps = ((src, src_own), (ping, WIDE), (pong, WIDE), (ping, WIDE), (dst, dst_own))
        for n in range(4):
            reach = margin - 1 - n
            source, source_own = steps[n]
            target, target_own = steps[n + 1]
            sweep(
                source,
                source_own,
                target,
                target_own,
                kind,
                -reach,
                ROWS + reach,
                add if n == 3 else None,
                add_own,
            )

    def project(src, src_own, out, upper, lower):
        def body(s, c):
            for base, sub in ((upper, 0), (lower, SUB // 2)):
                for h in range(HALVES):
                    value = [
                        src[base + s + src_own, h, pl.ds(SUB * g, SUB), :] for g in range(GROUPS)
                    ]
                    for n in range(NT):
                        total = value[0] * pert_t[n, base + s, h, pl.ds(0, SUB), :]
                        for g in range(1, GROUPS):
                            total = (
                                total + value[g] * pert_t[n, base + s, h, pl.ds(SUB * g, SUB), :]
                            )
                        out[m, HALVES * n + h, pl.ds(s + sub, 1), :] = jnp.sum(
                            total, axis=0, keepdims=True
                        )
            return c

        lax.fori_loop(0, SUB // 2, body, 0)

    def to_members(out, first):
        copies = []
        for k in range(1, MEM_COUNT):
            copies.append(
                pltpu.make_async_remote_copy(
                    src_ref=out.at[m],
                    dst_ref=out.at[m],
                    send_sem=red_send.at[first, k],
                    recv_sem=red_recv.at[first, k],
                    device_id=(lax.rem(m + k, MEM_COUNT), t),
                    device_id_type=MESH,
                )
            )
        for copy in copies:
            copy.start()
        return copies

    def wait_members(out, first):
        for k in range(1, MEM_COUNT):
            pltpu.make_async_remote_copy(
                src_ref=out.at[m],
                dst_ref=out.at[lax.rem(m + MEM_COUNT - k, MEM_COUNT)],
                send_sem=red_send.at[first, k],
                recv_sem=red_recv.at[first, k],
                device_id=(lax.rem(m + k, MEM_COUNT), t),
                device_id_type=MESH,
            ).wait_recv()

    def total_of(out, index):
        total = out[0, index]
        for k in range(1, MEM_COUNT):
            total = total + out[k, index]
        return total

    def observed(which, h, n, edge):
        upper = obs_in[which, h, pl.ds(ROWS * n, SUB), :]
        lower = obs_in[which, h, pl.ds(ROWS * n + SUB, SUB), :]
        return jnp.where(low_sub, upper, lower) if edge else jnp.where(low_sub, lower, upper)

    def pull_back(dst, dst_own, block, upper, lower):
        def body(s, c):
            for base, sub in ((upper, 0), (lower, SUB // 2)):
                for h in range(HALVES):
                    w = [
                        mis[block, HALVES * n + h, pl.ds(s + sub, SUB, stride=0), :]
                        for n in range(NT)
                    ]
                    for g in range(GROUPS):
                        part = pl.ds(SUB * g, SUB)
                        value = w[0] * pert_t[0, base + s, h, part, :]
                        for n in range(1, NT):
                            value = value + w[n] * pert_t[n, base + s, h, part, :]
                        dst[base + s + dst_own, h, part, :] = value
            return c

        lax.fori_loop(0, SUB // 2, body, 0)

    for copy in ctrl_copies:
        copy.wait()

    four_sweeps(field, NEAR, pong, WIDE, FORWARD, NEAR)
    project(pong, WIDE, edge_1, 0, 12)
    sent_e1 = to_members(edge_1, 0)
    project(pong, WIDE, mid_1, 8, 4)
    sent_m1 = to_members(mid_1, 1)
    for block, out, upper, lower in ((0, edge_1, 0, 12), (1, mid_1, 8, 4)):
        wait_members(out, block)
        for n in range(NT):
            for h in range(HALVES):
                mis[block, HALVES * n + h] = observed(1, h, n, block == 0) * (
                    total_of(out, HALVES * n + h) - observed(0, h, n, block == 0)
                )
        pull_back(pulled, WIDE, block, upper, lower)

    pull_copies = to_neighbours(rows_of(pulled), WIDE, WIDE, 4)
    for copy in pull_copies:
        copy.wait()
    four_sweeps(pulled, WIDE, grad, NEAR, ADJOINT, WIDE, add=field, add_own=NEAR)

    def square(r, total):
        for h in range(HALVES):
            for g in range(GROUPS):
                x = grad[r + NEAR, h, pl.ds(SUB * g, SUB), :]
                grad_nat[h, pl.ds(SUB * g * ROWS + r, SUB, stride=ROWS), :] = x
                total = total + x * x
        return total

    edge_2[m, NT * HALVES] = lax.fori_loop(
        0, ROWS, square, jnp.zeros((SUB, LANES), jnp.float32)
    )
    stores = [
        pltpu.make_async_copy(
            grad_nat.at[h], grad_out.at[:, pl.ds(h * LANES, LANES)], out_sem.at[h]
        )
        for h in range(HALVES)
    ]
    for copy in stores:
        copy.start()

    four_sweeps(grad, NEAR, pong, WIDE, FORWARD, NEAR)
    project(pong, WIDE, edge_2, 0, 12)
    sent_e2 = to_members(edge_2, 2)
    project(pong, WIDE, mid_2, 8, 4)
    sent_m2 = to_members(mid_2, 3)
    observed_sum = jnp.zeros((SUB, LANES), jnp.float32)
    last_copies = []
    for block, out, upper, lower in ((0, edge_2, 0, 12), (1, mid_2, 8, 4)):
        wait_members(out, 2 + block)
        for n in range(NT):
            for h in range(HALVES):
                image = total_of(out, HALVES * n + h)
                weighted = observed(1, h, n, block == 0) * image
                mis[2 + block, HALVES * n + h] = weighted
                observed_sum = observed_sum + image * weighted
        pull_back(pulled_2, NEAR, 2 + block, upper, lower)
        if block == 0:
            last_copies = to_neighbours(rows_of(pulled_2), NEAR, NEAR, 6)
    squares = total_of(edge_2, NT * HALVES)

    scal[t] = jnp.where(
        low_sub,
        jnp.broadcast_to(jnp.sum(squares, axis=0, keepdims=True), (SUB, LANES)),
        jnp.broadcast_to(jnp.sum(observed_sum, axis=0, keepdims=True), (SUB, LANES)),
    )

    def scalar_copy(k, slot):
        return pltpu.make_async_remote_copy(
            src_ref=scal.at[t],
            dst_ref=scal.at[slot],
            send_sem=scal_send.at[k],
            recv_sem=scal_recv.at[k],
            device_id=(m, lax.rem(t + k, TILE_COUNT)),
            device_id_type=MESH,
        )

    def send_scalar(k, c):
        scalar_copy(k, t).start()
        return c

    lax.fori_loop(1, TILE_COUNT, send_scalar, 0)

    for copy in last_copies:
        copy.wait()
    four_sweeps(pulled_2, NEAR, pong, WIDE, ADJOINT, NEAR, add=grad, add_own=NEAR)

    def place_hess(r, c):
        for h in range(HALVES):
            for g in range(GROUPS):
                hess_nat[h, pl.ds(SUB * g * ROWS + r, SUB, stride=ROWS), :] = pong[
                    r + WIDE, h, pl.ds(SUB * g, SUB), :
                ]
        return c

    lax.fori_loop(0, ROWS, place_hess, 0, unroll=2)
    for h in range(HALVES):
        copy = pltpu.make_async_copy(
            hess_nat.at[h], hess_out.at[:, pl.ds(h * LANES, LANES)], out_sem.at[HALVES + h]
        )
        copy.start()
        stores.append(copy)

    def wait_scalar(k, c):
        copy = scalar_copy(k, lax.rem(t + TILE_COUNT - k, TILE_COUNT))
        copy.wait_recv()
        copy.wait_send()
        return c

    lax.fori_loop(1, TILE_COUNT, wait_scalar, 0)
    sums = lax.fori_loop(
        0, TILE_COUNT, lambda k, s: s + scal[k], jnp.zeros((SUB, LANES), jnp.float32)
    )
    both = jnp.sum(sums, axis=1, keepdims=True)
    all_squares = both[0:1]
    step_out[...] = all_squares / (all_squares + both[SUB // 2 : SUB // 2 + 1])

    for copies in (sent_e1, sent_m1, sent_e2, sent_m2):
        for copy in copies:
            copy.wait_send()
    for copy in stores:
        copy.wait()


def shards(perturbations, control, innovation, obs_weight, diffusion, advection, upwind):
    f32 = jnp.float32
    cells = MEMBERS * ROWS
    width = HALVES * LANES
    any_space = pl.BlockSpec(memory_space=pl.ANY)

    def lines(count):
        return pltpu.VMEM((count, HALVES, MEMBERS, LANES), f32)

    def sums(count):
        return pltpu.VMEM((MEM_COUNT, count, SUB, LANES), f32)

    gradient, hessian, step = pl.pallas_call(
        kernel,
        out_shape=(
            jax.ShapeDtypeStruct((cells, width), f32),
            jax.ShapeDtypeStruct((cells, width), f32),
            jax.ShapeDtypeStruct((1, 1), f32),
        ),
        in_specs=[any_space] * 7,
        out_specs=(any_space, any_space, pl.BlockSpec(memory_space=pltpu.VMEM)),
        scratch_shapes=[
            pltpu.VMEM((HALVES, cells, LANES), f32),
            pltpu.VMEM((NT * cells, width), jnp.bfloat16),
            pltpu.VMEM((HALVES, NT * cells, LANES), f32),
            pltpu.VMEM((NT, ROWS, HALVES, MEMBERS, LANES), f32),
            pltpu.VMEM((2, HALVES, ROWS, LANES), f32),
            pltpu.VMEM((HALVES, ROWS, LANES), jnp.int32),
            pltpu.VMEM((2, HALVES, NT * ROWS, LANES), f32),
            pltpu.VMEM((3, HALVES, EXT, LANES), f32),
            pltpu.VMEM((10, HALVES, EXT, LANES), f32),
            lines(ROWS + 2 * NEAR),
            lines(EXT),
            lines(EXT),
            lines(EXT),
            lines(ROWS + 2 * NEAR),
            lines(ROWS + 2 * NEAR),
            sums(NT * HALVES),
            sums(NT * HALVES),
            sums(NT * HALVES + 1),
            sums(NT * HALVES),
            pltpu.VMEM((4, NT * HALVES, SUB, LANES), f32),
            pltpu.VMEM((TILE_COUNT, SUB, LANES), f32),
            pltpu.VMEM((HALVES, cells, LANES), f32),
            pltpu.VMEM((HALVES, cells, LANES), f32),
            pltpu.SemaphoreType.DMA((13,)),
            pltpu.SemaphoreType.DMA((4,)),
            pltpu.SemaphoreType.DMA((8,)),
            pltpu.SemaphoreType.DMA((8,)),
            pltpu.SemaphoreType.DMA((4, MEM_COUNT)),
            pltpu.SemaphoreType.DMA((4, MEM_COUNT)),
            pltpu.SemaphoreType.DMA((TILE_COUNT,)),
            pltpu.SemaphoreType.DMA((TILE_COUNT,)),
        ],
        compiler_params=pltpu.CompilerParams(
            collective_id=0, has_side_effects=True, vmem_limit_bytes=63 << 20
        ),
    )(
        control.reshape(cells, width),
        perturbations.reshape(NT * cells, width),
        innovation.reshape(NT * ROWS, width),
        obs_weight.reshape(NT * ROWS, width),
        diffusion,
        advection,
        upwind,
    )
    return (
        gradient.reshape(control.shape),
        hessian.reshape(control.shape),
        step.reshape(()),
    )


def solution(mesh):
    return jax.shard_map(
        shards,
        mesh=mesh,
        in_specs=(
            P(None, "mem", "tile", None),
            P("mem", "tile", None),
            P(None, "tile", None),
            P(None, "tile", None),
            P("tile", None),
            P("tile", None),
            P("tile", None),
        ),
        out_specs=(P("mem", "tile", None), P("mem", "tile", None), P()),
        check_vma=False,
    )
```

```python
import functools

import jax
import jax.numpy as jnp
from jax import lax
from jax.experimental import pallas as pl
from jax.experimental.pallas import tpu as pltpu
from jax.sharding import PartitionSpec as P

MESH = pl.DeviceIdType.MESH
SUB = 8
LANES = 128
HALVES = 2
NT = 3
ROWS = 16
MEMBERS = 32
GROUPS = MEMBERS // SUB
MEM_COUNT = 8
TILE_COUNT = 32
WIDE = 8
EXT = ROWS + 2 * WIDE
NEAR = 4
PLANE = 4
FORWARD = 0
ADJOINT = 5


def kernel(
    ctrl,
    pert,
    innov,
    weight,
    diff,
    adv,
    upw,
    grad_out,
    hess_out,
    step_out,
    ctrl_nat,
    pert_half,
    pert_nat,
    pert_t,
    small_in,
    upw_in,
    obs_in,
    raw,
    coef,
    field,
    level_1,
    level_2,
    level_3,
    pulled,
    grad,
    pulled_2,
    result,
    edge_1,
    mid_1,
    edge_2,
    mid_2,
    mis,
    scal,
    grad_nat,
    hess_nat,
    in_sem,
    out_sem,
    halo_send,
    halo_recv,
    red_send,
    red_recv,
    scal_send,
    scal_recv,
    known_sem,
):
    t = lax.axis_index("tile")
    m = lax.axis_index("mem")

    def tile_at(k):
        return lax.rem(t + k + TILE_COUNT, TILE_COUNT)

    barrier = pltpu.get_barrier_semaphore()
    near = [tile_at(1), tile_at(-1), tile_at(PLANE), tile_at(-PLANE)]
    near += [(t // PLANE) * PLANE + lax.rem(t + k, PLANE) for k in range(1, PLANE)]
    greeted = [(m, other) for other in near]
    greeted += [(lax.rem(m + k, MEM_COUNT), t) for k in range(1, MEM_COUNT)]
    for device in greeted:
        pl.semaphore_signal(barrier, inc=1, device_id=device, device_id_type=MESH)

    def tell():
        for n, k in enumerate((PLANE, -PLANE)):
            pl.semaphore_signal(
                known_sem.at[n], inc=1, device_id=(m, tile_at(k)), device_id_type=MESH
            )

    def hear():
        for n in range(2):
            pl.semaphore_wait(known_sem.at[n], 1)

    loads = []
    for h in range(HALVES):
        cols = pl.ds(h * LANES, LANES)
        loads.append((ctrl.at[:, cols], ctrl_nat.at[h]))
        loads.append((diff.at[:, cols], small_in.at[0, h]))
        loads.append((adv.at[:, cols], small_in.at[1, h]))
        loads.append((upw.at[:, cols], upw_in.at[h]))
    first_loads = len(loads)
    loads.append((pert, pert_half))
    for h in range(HALVES):
        cols = pl.ds(h * LANES, LANES)
        loads.append((innov.at[:, cols], obs_in.at[0, h]))
        loads.append((weight.at[:, cols], obs_in.at[1, h]))
    loads = [
        pltpu.make_async_copy(src, dst, in_sem.at[n]) for n, (src, dst) in enumerate(loads)
    ]
    for copy in loads:
        copy.start()

    lane = lax.broadcasted_iota(jnp.int32, (SUB, LANES), 1)
    sub = lax.broadcasted_iota(jnp.int32, (SUB, LANES), 0)
    low_sub = sub < SUB // 2
    at_last = lane == LANES - 1
    at_first = lane == 0

    for copy in loads[:first_loads]:
        copy.wait()

    def place_control(r, c):
        for h in range(HALVES):
            for g in range(GROUPS):
                field[r + WIDE, h, pl.ds(SUB * g, SUB), :] = ctrl_nat[
                    h, pl.ds(SUB * g * ROWS + r, SUB, stride=ROWS), :
                ]
        return c

    lax.fori_loop(0, ROWS, place_control, 0, unroll=4)
    for h in range(HALVES):
        raw[0, h, pl.ds(WIDE, ROWS), :] = small_in[0, h]
        raw[1, h, pl.ds(WIDE, ROWS), :] = small_in[1, h]
        raw[2, h, pl.ds(WIDE, ROWS), :] = jnp.where(upw_in[h] == 1, 1.0, 0.0)

    def to_neighbours(buffer, low, high, depth, first):
        copies = []
        for n, (row, shift, dest) in enumerate(
            ((low, ROWS, tile_at(-1)), (high, -ROWS, tile_at(1)))
        ):
            copies.append(
                pltpu.make_async_remote_copy(
                    src_ref=buffer(row + WIDE, depth),
                    dst_ref=buffer(row + WIDE + shift, depth),
                    send_sem=halo_send.at[first + n],
                    recv_sem=halo_recv.at[first + n],
                    device_id=(m, dest),
                    device_id_type=MESH,
                )
            )
        for copy in copies:
            copy.start()
        return copies

    def rows_of(ref):
        return lambda start, count: ref.at[pl.ds(start, count)]

    pl.semaphore_wait(barrier, len(greeted))

    ctrl_copies = to_neighbours(rows_of(field), 0, ROWS - NEAR, NEAR, 2)
    coef_copies = to_neighbours(
        lambda start, count: raw.at[:, :, pl.ds(start, count), :], 0, ROWS - WIDE, WIDE, 0
    )
    tell()

    def shifted(pair):
        lanes = lax.broadcasted_iota(jnp.int32, pair[0].shape, 1)
        right = [pltpu.roll(x, LANES - 1, 1) for x in pair]
        left = [pltpu.roll(x, 1, 1) for x in pair]
        right = [
            jnp.where(lanes == LANES - 1, right[1], right[0]),
            jnp.where(lanes == LANES - 1, 0.0, right[1]),
        ]
        left = [
            jnp.where(lanes == 0, 0.0, left[0]),
            jnp.where(lanes == 0, left[0], left[1]),
        ]
        return right, left

    top_tile = t == 0
    bottom_tile = t == TILE_COUNT - 1

    def forward_coef(block):
        rows = pl.ds(SUB * block, SUB)
        for h in range(HALVES):
            k = raw[0, h, rows, :]
            a = raw[1, h, rows, :]
            u = raw[2, h, rows, :]
            below = k + a * u
            above = k + a * (1.0 - u)
            if block == 1:
                above = jnp.where(jnp.logical_and(sub == 0, top_tile), 0.0, above)
            if block == 2:
                below = jnp.where(jnp.logical_and(sub == SUB - 1, bottom_tile), 0.0, below)
            coef[FORWARD + 0, h, rows, :] = 1.0 - 4.0 * k - a
            coef[FORWARD + 1, h, rows, :] = below
            coef[FORWARD + 2, h, rows, :] = above
            coef[FORWARD + 3, h, rows, :] = jnp.where(at_last, 0.0, k) if h else k
            coef[FORWARD + 4, h, rows, :] = k if h else jnp.where(at_first, 0.0, k)

    def adjoint_coef():
        row = lax.broadcasted_iota(jnp.int32, (EXT, LANES), 0)
        top = jnp.logical_and(row == WIDE, top_tile)
        bottom = jnp.logical_and(row == WIDE + ROWS - 1, bottom_tile)
        right, left = shifted([raw[0, h] for h in range(HALVES)])
        for h in range(HALVES):
            k = raw[0, h]
            a = raw[1, h]
            u = raw[2, h]
            below = k + a * u
            above = k + a * (1.0 - u)
            coef[ADJOINT + 0, h] = 1.0 - 4.0 * k - a
            coef[ADJOINT + 1, h] = jnp.where(bottom, 0.0, pltpu.roll(above, EXT - 1, 0))
            coef[ADJOINT + 2, h] = jnp.where(top, 0.0, pltpu.roll(below, 1, 0))
            coef[ADJOINT + 3, h] = right[h]
            coef[ADJOINT + 4, h] = left[h]

    def four_sweeps(source, target, kind, parts, add=None, together=GROUPS):
        chain = (source, level_1, level_2, level_3, target)

        def body(q, c):
            for n in range(4):
                src, dst = chain[n], chain[n + 1]
                for first, last in parts[n]:
                    for r in range(first, last):
                        f = [
                            [
                                coef[kind + i, h, pl.ds(r + WIDE, SUB, stride=0), :]
                                for h in range(HALVES)
                            ]
                            for i in range(5)
                        ]
                        for g in range(together):
                            part = pl.ds(SUB * g, SUB)
                            if together < GROUPS:
                                part = pl.ds(
                                    pl.multiple_of(SUB * (together * q + g), SUB), SUB
                                )
                            above, centre, below = [
                                [src[r + WIDE + d, h, part, :] for h in range(HALVES)]
                                for d in range(-1, 2)
                            ]
                            right = [pltpu.roll(x, LANES - 1, 1) for x in centre]
                            left = [pltpu.roll(x, 1, 1) for x in centre]
                            right = [jnp.where(at_last, right[1], right[0]), right[1]]
                            left = [left[0], jnp.where(at_first, left[0], left[1])]
                            for h in range(HALVES):
                                value = (f[0][h] * centre[h] + f[1][h] * below[h]) + (
                                    f[2][h] * above[h]
                                    + (f[3][h] * right[h] + f[4][h] * left[h])
                                )
                                if add is not None and n == 3:
                                    value = value + add[r + WIDE, h, part, :]
                                dst[r + WIDE, h, part, :] = value
            return c

        if together == GROUPS:
            body(0, 0)
        else:
            lax.fori_loop(0, GROUPS // together, body, 0)

    inner = [[(n, ROWS - n)] for n in range(1, 5)]
    near_rim = [[(n - 4, n), (ROWS - n, ROWS + 4 - n)] for n in range(1, 5)]
    wide_rim = [[(n - 8, n), (ROWS - n, ROWS + 8 - n)] for n in range(1, 5)]
    core = [[(5, 11)], [(6, 10)], [(7, 9)], []]
    core_rim = [[(n - 4, 4 + n), (12 - n, 20 - n)] for n in range(1, 4)] + [[(0, ROWS)]]

    edge_rows = (0, 1, 2, 3, 12, 13, 14, 15)
    mid_rows = (8, 9, 10, 11, 4, 5, 6, 7)

    def project(rows, out):
        for s, r in enumerate(rows):
            for h in range(HALVES):
                value = [result[r + WIDE, h, pl.ds(SUB * g, SUB), :] for g in range(GROUPS)]
                for n in range(NT):
                    total = value[0] * pert_t[n, r, h, pl.ds(0, SUB), :]
                    for g in range(1, GROUPS):
                        total = total + value[g] * pert_t[n, r, h, pl.ds(SUB * g, SUB), :]
                    out[m, HALVES * n + h, pl.ds(s, 1), :] = jnp.sum(
                        total, axis=0, keepdims=True
                    )

    def to_members(out, first):
        copies = []
        for k in range(1, MEM_COUNT):
            copies.append(
                pltpu.make_async_remote_copy(
                    src_ref=out.at[m],
                    dst_ref=out.at[m],
                    send_sem=red_send.at[first, k],
                    recv_sem=red_recv.at[first, k],
                    device_id=(lax.rem(m + k, MEM_COUNT), t),
                    device_id_type=MESH,
                )
            )
        for copy in copies:
            copy.start()
        return copies

    def wait_members(out, first):
        for k in range(1, MEM_COUNT):
            pltpu.make_async_remote_copy(
                src_ref=out.at[m],
                dst_ref=out.at[lax.rem(m + MEM_COUNT - k, MEM_COUNT)],
                send_sem=red_send.at[first, k],
                recv_sem=red_recv.at[first, k],
                device_id=(lax.rem(m + k, MEM_COUNT), t),
                device_id_type=MESH,
            ).wait_recv()

    def total_of(out, index):
        total = [out[k, index] for k in range(MEM_COUNT)]
        while len(total) > 1:
            total = [a + b for a, b in zip(total[::2], total[1::2])]
        return total[0]

    def observed(which, h, n, edge):
        upper = obs_in[which, h, pl.ds(ROWS * n, SUB), :]
        lower = obs_in[which, h, pl.ds(ROWS * n + SUB, SUB), :]
        return jnp.where(low_sub, upper, lower) if edge else jnp.where(low_sub, lower, upper)

    def pull_back(dst, block, rows):
        for s, r in enumerate(rows):
            for h in range(HALVES):
                w = [
                    mis[block, HALVES * n + h, pl.ds(s, SUB, stride=0), :] for n in range(NT)
                ]
                for g in range(GROUPS):
                    part = pl.ds(SUB * g, SUB)
                    value = w[0] * pert_t[0, r, h, part, :]
                    for n in range(1, NT):
                        value = value + w[n] * pert_t[n, r, h, part, :]
                    dst[r + WIDE, h, part, :] = value

    def place(src, dst, rows):
        for r in rows:
            for h in range(HALVES):
                for g in range(GROUPS):
                    dst[h, pl.ds(SUB * g * ROWS + r, SUB, stride=ROWS), :] = src[
                        r + WIDE, h, pl.ds(SUB * g, SUB), :
                    ]

    forward_coef(1)
    forward_coef(2)
    for copy in loads[first_loads:]:
        copy.wait()

    def widen(q, c):
        rows = pl.ds(pl.multiple_of(q * ROWS, ROWS), ROWS)
        for h in range(HALVES):
            pert_nat[h, rows, :] = pert_half[rows, pl.ds(h * LANES, LANES)].astype(jnp.float32)
        return c

    lax.fori_loop(0, NT * MEMBERS, widen, 0, unroll=8)

    def place_pert(r, c):
        for n in range(NT):
            for h in range(HALVES):
                for g in range(GROUPS):
                    pert_t[n, r, h, pl.ds(SUB * g, SUB), :] = pert_nat[
                        h, pl.ds((n * MEMBERS + SUB * g) * ROWS + r, SUB, stride=ROWS), :
                    ]
        return c

    lax.fori_loop(0, ROWS, place_pert, 0, unroll=2)

    four_sweeps(field, result, FORWARD, inner, together=2)
    project(mid_rows, mid_1)
    sent_m1 = to_members(mid_1, 1)

    for copy in coef_copies + ctrl_copies:
        copy.wait()
    forward_coef(0)
    forward_coef(3)
    four_sweeps(field, result, FORWARD, near_rim)
    project(edge_rows, edge_1)
    sent_e1 = to_members(edge_1, 0)
    hear()
    tell()
    adjoint_coef()

    def misfit(block, out):
        for n in range(NT):
            for h in range(HALVES):
                mis[block, HALVES * n + h] = observed(1, h, n, block == 0) * (
                    total_of(out, HALVES * n + h) - observed(0, h, n, block == 0)
                )

    wait_members(mid_1, 1)
    misfit(1, mid_1)
    pull_back(pulled, 1, mid_rows)
    pull_copies = to_neighbours(rows_of(pulled), NEAR, ROWS - 2 * NEAR, NEAR, 4)
    wait_members(edge_1, 0)
    misfit(0, edge_1)
    pull_back(pulled, 0, edge_rows)
    pull_copies += to_neighbours(rows_of(pulled), 0, ROWS - NEAR, NEAR, 6)
    hear()
    tell()

    four_sweeps(pulled, grad, ADJOINT, inner, add=field, together=2)
    four_sweeps(grad, result, FORWARD, core, together=2)
    for copy in pull_copies:
        copy.wait()
    four_sweeps(pulled, grad, ADJOINT, wide_rim, add=field, together=2)
    four_sweeps(grad, result, FORWARD, core_rim, together=2)
    project(edge_rows, edge_2)
    sent_e2 = to_members(edge_2, 2)
    squares = []
    for r in range(ROWS):
        for h in range(HALVES):
            for g in range(GROUPS):
                x = grad[r + WIDE, h, pl.ds(SUB * g, SUB), :]
                squares.append(x * x)
    while len(squares) > 1:
        squares = [a + b for a, b in zip(squares[::2], squares[1::2])]
    mid_2[m, NT * HALVES] = squares[0]
    project(mid_rows, mid_2)
    sent_m2 = to_members(mid_2, 3)
    hear()
    tell()
    place(grad, grad_nat, range(ROWS))
    stores = []

    def store(src, dst, first):
        for h in range(HALVES):
            copy = pltpu.make_async_copy(
                src.at[h], dst.at[:, pl.ds(h * LANES, LANES)], out_sem.at[first + h]
            )
            copy.start()
            stores.append(copy)

    store(grad_nat, grad_out, 0)

    def weigh(block, out, total):
        for n in range(NT):
            for h in range(HALVES):
                image = total_of(out, HALVES * n + h)
                weighted = observed(1, h, n, block == 0) * image
                mis[2 + block, HALVES * n + h] = weighted
                total = total + image * weighted
        return total

    wait_members(edge_2, 2)
    observed_sum = weigh(0, edge_2, jnp.zeros((SUB, LANES), jnp.float32))
    pull_back(pulled_2, 2, edge_rows)
    last_copies = to_neighbours(rows_of(pulled_2), 0, ROWS - NEAR, NEAR, 8)
    hear()
    wait_members(mid_2, 3)
    observed_sum = weigh(1, mid_2, observed_sum)
    squares = total_of(mid_2, NT * HALVES)

    scal[t] = jnp.where(
        low_sub,
        jnp.broadcast_to(jnp.sum(squares, axis=0, keepdims=True), (SUB, LANES)),
        jnp.broadcast_to(jnp.sum(observed_sum, axis=0, keepdims=True), (SUB, LANES)),
    )

    def scalar_copy(k, slot):
        return pltpu.make_async_remote_copy(
            src_ref=scal.at[t],
            dst_ref=scal.at[slot],
            send_sem=scal_send.at[k],
            recv_sem=scal_recv.at[k],
            device_id=(m, lax.rem(t + k, TILE_COUNT)),
            device_id_type=MESH,
        )

    def send_scalar(k, c):
        scalar_copy(k, t).start()
        return c

    lax.fori_loop(1, TILE_COUNT, send_scalar, 0)

    pull_back(pulled_2, 3, mid_rows)
    four_sweeps(pulled_2, result, ADJOINT, inner, add=grad, together=2)
    place(result, hess_nat, mid_rows)
    for copy in last_copies:
        copy.wait()
    four_sweeps(pulled_2, result, ADJOINT, near_rim, add=grad)
    place(result, hess_nat, edge_rows)
    store(hess_nat, hess_out, HALVES)

    def wait_scalar(k, c):
        copy = scalar_copy(k, lax.rem(t + TILE_COUNT - k, TILE_COUNT))
        copy.wait_recv()
        copy.wait_send()
        return c

    lax.fori_loop(1, TILE_COUNT, wait_scalar, 0)
    sums = [scal[k] for k in range(TILE_COUNT)]
    while len(sums) > 1:
        sums = [a + b for a, b in zip(sums[::2], sums[1::2])]
    both = jnp.sum(sums[0], axis=1, keepdims=True)
    all_squares = both[0:1]
    step_out[...] = all_squares / (all_squares + both[SUB // 2 : SUB // 2 + 1])

    for copies in (sent_e1, sent_m1, sent_e2, sent_m2):
        for copy in copies:
            copy.wait_send()
    for copy in stores:
        copy.wait()


def shards(perturbations, control, innovation, obs_weight, diffusion, advection, upwind):
    f32 = jnp.float32
    cells = MEMBERS * ROWS
    width = HALVES * LANES
    any_space = pl.BlockSpec(memory_space=pl.ANY)

    def lines(count):
        return pltpu.VMEM((count, HALVES, MEMBERS, LANES), f32)

    def sums(count):
        return pltpu.VMEM((MEM_COUNT, count, SUB, LANES), f32)

    gradient, hessian, step = pl.pallas_call(
        kernel,
        out_shape=(
            jax.ShapeDtypeStruct((cells, width), f32),
            jax.ShapeDtypeStruct((cells, width), f32),
            jax.ShapeDtypeStruct((1, 1), f32),
        ),
        in_specs=[any_space] * 7,
        out_specs=(any_space, any_space, pl.BlockSpec(memory_space=pltpu.VMEM)),
        scratch_shapes=[
            pltpu.VMEM((HALVES, cells, LANES), f32),
            pltpu.VMEM((NT * cells, width), jnp.bfloat16),
            pltpu.VMEM((HALVES, NT * cells, LANES), f32),
            pltpu.VMEM((NT, ROWS, HALVES, MEMBERS, LANES), f32),
            pltpu.VMEM((2, HALVES, ROWS, LANES), f32),
            pltpu.VMEM((HALVES, ROWS, LANES), jnp.int32),
            pltpu.VMEM((2, HALVES, NT * ROWS, LANES), f32),
            pltpu.VMEM((3, HALVES, EXT, LANES), f32),
            pltpu.VMEM((10, HALVES, EXT, LANES), f32),
            *[lines(EXT)] * 8,
            sums(NT * HALVES),
            sums(NT * HALVES),
            sums(NT * HALVES),
            sums(NT * HALVES + 1),
            pltpu.VMEM((4, NT * HALVES, SUB, LANES), f32),
            pltpu.VMEM((TILE_COUNT, SUB, LANES), f32),
            pltpu.VMEM((HALVES, cells, LANES), f32),
            pltpu.VMEM((HALVES, cells, LANES), f32),
            pltpu.SemaphoreType.DMA((13,)),
            pltpu.SemaphoreType.DMA((4,)),
            pltpu.SemaphoreType.DMA((10,)),
            pltpu.SemaphoreType.DMA((10,)),
            pltpu.SemaphoreType.DMA((4, MEM_COUNT)),
            pltpu.SemaphoreType.DMA((4, MEM_COUNT)),
            pltpu.SemaphoreType.DMA((TILE_COUNT,)),
            pltpu.SemaphoreType.DMA((TILE_COUNT,)),
            pltpu.SemaphoreType.REGULAR((2,)),
        ],
        compiler_params=pltpu.CompilerParams(
            collective_id=0, has_side_effects=True, vmem_limit_bytes=63 << 20
        ),
    )(
        control.reshape(cells, width),
        perturbations.reshape(NT * cells, width),
        innovation.reshape(NT * ROWS, width),
        obs_weight.reshape(NT * ROWS, width),
        diffusion,
        advection,
        upwind,
    )
    return (
        gradient.reshape(control.shape),
        hessian.reshape(control.shape),
        step.reshape(()),
    )


def solution(mesh):
    return jax.shard_map(
        shards,
        mesh=mesh,
        in_specs=(
            P(None, "mem", "tile", None),
            P("mem", "tile", None),
            P(None, "tile", None),
            P(None, "tile", None),
            P("tile", None),
            P("tile", None),
            P("tile", None),
        ),
        out_specs=(P("mem", "tile", None), P("mem", "tile", None), P()),
        check_vma=False,
    )
```

```python
import functools

import jax
import jax.numpy as jnp
from jax import lax
from jax.experimental import pallas as pl
from jax.experimental.pallas import tpu as pltpu
from jax.sharding import PartitionSpec as P

MESH = pl.DeviceIdType.MESH
SUB = 8
LANES = 128
HALVES = 2
NT = 3
ROWS = 16
MEMBERS = 32
GROUPS = MEMBERS // SUB
HALF = MEMBERS // 2
MEM_COUNT = 8
TILE_COUNT = 32
WIDE = 8
EXT = ROWS + 2 * WIDE
NEAR = 4
PLANE = 4
FORWARD = 0
ADJOINT = 5


def kernel(
    ctrl,
    pert,
    innov,
    weight,
    diff,
    adv,
    upw,
    grad_out,
    hess_out,
    step_out,
    ctrl_nat,
    pert_half,
    pert_nat,
    pert_t,
    small_in,
    upw_in,
    obs_in,
    raw,
    coef,
    field,
    level_1,
    level_2,
    level_3,
    pulled,
    grad,
    pulled_2,
    result,
    edge_1,
    mid_1,
    edge_2,
    mid_2,
    mis,
    scal,
    grad_nat,
    hess_nat,
    in_sem,
    out_sem,
    halo_send,
    halo_recv,
    red_send,
    red_recv,
    scal_send,
    scal_recv,
    known_sem,
):
    t = lax.axis_index("tile")
    m = lax.axis_index("mem")

    def tile_at(k):
        return lax.rem(t + k + TILE_COUNT, TILE_COUNT)

    barrier = pltpu.get_barrier_semaphore()
    near = [tile_at(1), tile_at(-1), tile_at(PLANE), tile_at(-PLANE)]
    near += [(t // PLANE) * PLANE + lax.rem(t + k, PLANE) for k in range(1, PLANE)]
    greeted = [(m, other) for other in near]
    greeted += [(lax.rem(m + k, MEM_COUNT), t) for k in range(1, MEM_COUNT)]
    for device in greeted:
        pl.semaphore_signal(barrier, inc=1, device_id=device, device_id_type=MESH)

    def tell():
        for n, k in enumerate((PLANE, -PLANE)):
            pl.semaphore_signal(
                known_sem.at[n], inc=1, device_id=(m, tile_at(k)), device_id_type=MESH
            )

    def hear():
        for n in range(2):
            pl.semaphore_wait(known_sem.at[n], 1)

    loads = []
    for h in range(HALVES):
        cols = pl.ds(h * LANES, LANES)
        loads.append((ctrl.at[:, cols], ctrl_nat.at[h]))
        loads.append((diff.at[:, cols], small_in.at[0, h]))
        loads.append((adv.at[:, cols], small_in.at[1, h]))
        loads.append((upw.at[:, cols], upw_in.at[h]))
    first_loads = len(loads)
    loads.append((pert, pert_half))
    for h in range(HALVES):
        cols = pl.ds(h * LANES, LANES)
        loads.append((innov.at[:, cols], obs_in.at[0, h]))
        loads.append((weight.at[:, cols], obs_in.at[1, h]))
    loads = [
        pltpu.make_async_copy(src, dst, in_sem.at[n]) for n, (src, dst) in enumerate(loads)
    ]
    for copy in loads:
        copy.start()

    lane = lax.broadcasted_iota(jnp.int32, (SUB, LANES), 1)
    sub = lax.broadcasted_iota(jnp.int32, (SUB, LANES), 0)
    low_sub = sub < SUB // 2
    at_last = lane == LANES - 1
    at_first = lane == 0

    for copy in loads[:first_loads]:
        copy.wait()

    def place_control(r, c):
        for h in range(HALVES):
            for g in range(GROUPS):
                field[r + WIDE, h, pl.ds(SUB * g, SUB), :] = ctrl_nat[
                    h, pl.ds(SUB * g * ROWS + r, SUB, stride=ROWS), :
                ]
        return c

    lax.fori_loop(0, ROWS, place_control, 0, unroll=4)
    for h in range(HALVES):
        raw[0, h, pl.ds(WIDE, ROWS), :] = small_in[0, h]
        raw[1, h, pl.ds(WIDE, ROWS), :] = small_in[1, h]
        raw[2, h, pl.ds(WIDE, ROWS), :] = jnp.where(upw_in[h] == 1, 1.0, 0.0)

    def half_rows(ref, half):
        part = pl.ds(HALF * half, HALF)
        return lambda start, count: ref.at[pl.ds(start, count), :, part, :]

    def to_neighbours(buffer, low, high, depth, first):
        copies = []
        for n, (row, shift, dest) in enumerate(
            ((low, ROWS, tile_at(-1)), (high, -ROWS, tile_at(1)))
        ):
            copies.append(
                pltpu.make_async_remote_copy(
                    src_ref=buffer(row + WIDE, depth),
                    dst_ref=buffer(row + WIDE + shift, depth),
                    send_sem=halo_send.at[first + n],
                    recv_sem=halo_recv.at[first + n],
                    device_id=(m, dest),
                    device_id_type=MESH,
                )
            )
        for copy in copies:
            copy.start()
        return copies

    pl.semaphore_wait(barrier, len(greeted))

    coef_copies = to_neighbours(
        lambda start, count: raw.at[:, :, pl.ds(start, count), :], 0, ROWS - WIDE, WIDE, 0
    )
    ctrl_copies = [
        to_neighbours(half_rows(field, q), 0, ROWS - NEAR, NEAR, 2 + 2 * q) for q in range(2)
    ]
    tell()

    def shifted(pair):
        lanes = lax.broadcasted_iota(jnp.int32, pair[0].shape, 1)
        right = [pltpu.roll(x, LANES - 1, 1) for x in pair]
        left = [pltpu.roll(x, 1, 1) for x in pair]
        right = [
            jnp.where(lanes == LANES - 1, right[1], right[0]),
            jnp.where(lanes == LANES - 1, 0.0, right[1]),
        ]
        left = [
            jnp.where(lanes == 0, 0.0, left[0]),
            jnp.where(lanes == 0, left[0], left[1]),
        ]
        return right, left

    top_tile = t == 0
    bottom_tile = t == TILE_COUNT - 1

    def forward_coef(block):
        rows = pl.ds(SUB * block, SUB)
        for h in range(HALVES):
            k = raw[0, h, rows, :]
            a = raw[1, h, rows, :]
            u = raw[2, h, rows, :]
            below = k + a * u
            above = k + a * (1.0 - u)
            if block == 1:
                above = jnp.where(jnp.logical_and(sub == 0, top_tile), 0.0, above)
            if block == 2:
                below = jnp.where(jnp.logical_and(sub == SUB - 1, bottom_tile), 0.0, below)
            coef[FORWARD + 0, h, rows, :] = 1.0 - 4.0 * k - a
            coef[FORWARD + 1, h, rows, :] = below
            coef[FORWARD + 2, h, rows, :] = above
            coef[FORWARD + 3, h, rows, :] = jnp.where(at_last, 0.0, k) if h else k
            coef[FORWARD + 4, h, rows, :] = k if h else jnp.where(at_first, 0.0, k)

    def adjoint_coef():
        row = lax.broadcasted_iota(jnp.int32, (EXT, LANES), 0)
        top = jnp.logical_and(row == WIDE, top_tile)
        bottom = jnp.logical_and(row == WIDE + ROWS - 1, bottom_tile)
        right, left = shifted([raw[0, h] for h in range(HALVES)])
        for h in range(HALVES):
            k = raw[0, h]
            a = raw[1, h]
            u = raw[2, h]
            below = k + a * u
            above = k + a * (1.0 - u)
            coef[ADJOINT + 0, h] = 1.0 - 4.0 * k - a
            coef[ADJOINT + 1, h] = jnp.where(bottom, 0.0, pltpu.roll(above, EXT - 1, 0))
            coef[ADJOINT + 2, h] = jnp.where(top, 0.0, pltpu.roll(below, 1, 0))
            coef[ADJOINT + 3, h] = right[h]
            coef[ADJOINT + 4, h] = left[h]

    def four_sweeps(source, target, kind, parts, add=None, only=None):
        chain = (source, level_1, level_2, level_3, target)
        together = GROUPS // 2

        def body(q, c):
            for n in range(4):
                src, dst = chain[n], chain[n + 1]
                for first, last in parts[n]:
                    for r in range(first, last):
                        f = [
                            [
                                coef[kind + i, h, pl.ds(r + WIDE, SUB, stride=0), :]
                                for h in range(HALVES)
                            ]
                            for i in range(5)
                        ]
                        for g in range(together):
                            part = SUB * (together * q + g)
                            part = pl.ds(
                                part if only is not None else pl.multiple_of(part, SUB), SUB
                            )
                            above, centre, below = [
                                [src[r + WIDE + d, h, part, :] for h in range(HALVES)]
                                for d in range(-1, 2)
                            ]
                            right = [pltpu.roll(x, LANES - 1, 1) for x in centre]
                            left = [pltpu.roll(x, 1, 1) for x in centre]
                            right = [jnp.where(at_last, right[1], right[0]), right[1]]
                            left = [left[0], jnp.where(at_first, left[0], left[1])]
                            for h in range(HALVES):
                                value = (f[0][h] * centre[h] + f[1][h] * below[h]) + (
                                    f[2][h] * above[h]
                                    + (f[3][h] * right[h] + f[4][h] * left[h])
                                )
                                if add is not None and n == 3:
                                    value = value + add[r + WIDE, h, part, :]
                                dst[r + WIDE, h, part, :] = value
            return c

        if only is not None:
            body(only, 0)
        else:
            lax.fori_loop(0, 2, body, 0)

    inner = [[(n, ROWS - n)] for n in range(1, 5)]
    near_rim = [[(n - 4, n), (ROWS - n, ROWS + 4 - n)] for n in range(1, 5)]
    wide_rim = [[(n - 8, n), (ROWS - n, ROWS + 8 - n)] for n in range(1, 5)]
    core = [[(5, 11)], [(6, 10)], [(7, 9)], []]
    core_edge = [[(-3, 5), (11, 19)], [(-2, 6), (10, 18)], [(-1, 5), (11, 17)], [(0, 4), (12, 16)]]
    core_mid = [[], [], [(5, 7), (9, 11)], [(4, 12)]]

    edge_rows = (0, 1, 2, 3, 12, 13, 14, 15)
    mid_rows = (8, 9, 10, 11, 4, 5, 6, 7)
    group_half = ((0, 1), (2, 3))

    def project(rows, out):
        for s, r in enumerate(rows):
            for h in range(HALVES):
                value = [result[r + WIDE, h, pl.ds(SUB * g, SUB), :] for g in range(GROUPS)]
                for n in range(NT):
                    total = value[0] * pert_t[n, r, h, pl.ds(0, SUB), :]
                    for g in range(1, GROUPS):
                        total = total + value[g] * pert_t[n, r, h, pl.ds(SUB * g, SUB), :]
                    out[m, HALVES * n + h, pl.ds(s, 1), :] = jnp.sum(
                        total, axis=0, keepdims=True
                    )

    def to_members(out, first):
        copies = []
        for k in range(1, MEM_COUNT):
            copies.append(
                pltpu.make_async_remote_copy(
                    src_ref=out.at[m],
                    dst_ref=out.at[m],
                    send_sem=red_send.at[first, k],
                    recv_sem=red_recv.at[first, k],
                    device_id=(lax.rem(m + k, MEM_COUNT), t),
                    device_id_type=MESH,
                )
            )
        for copy in copies:
            copy.start()
        return copies

    def wait_members(out, first):
        for k in range(1, MEM_COUNT):
            pltpu.make_async_remote_copy(
                src_ref=out.at[m],
                dst_ref=out.at[lax.rem(m + MEM_COUNT - k, MEM_COUNT)],
                send_sem=red_send.at[first, k],
                recv_sem=red_recv.at[first, k],
                device_id=(lax.rem(m + k, MEM_COUNT), t),
                device_id_type=MESH,
            ).wait_recv()

    def total_of(out, index):
        total = [out[k, index] for k in range(MEM_COUNT)]
        while len(total) > 1:
            total = [a + b for a, b in zip(total[::2], total[1::2])]
        return total[0]

    def observed(which, h, n, edge):
        upper = obs_in[which, h, pl.ds(ROWS * n, SUB), :]
        lower = obs_in[which, h, pl.ds(ROWS * n + SUB, SUB), :]
        return jnp.where(low_sub, upper, lower) if edge else jnp.where(low_sub, lower, upper)

    def pull_back(dst, block, rows, groups=range(GROUPS)):
        for s, r in enumerate(rows):
            for h in range(HALVES):
                w = [
                    mis[block, HALVES * n + h, pl.ds(s, SUB, stride=0), :] for n in range(NT)
                ]
                for g in groups:
                    part = pl.ds(SUB * g, SUB)
                    value = w[0] * pert_t[0, r, h, part, :]
                    for n in range(1, NT):
                        value = value + w[n] * pert_t[n, r, h, part, :]
                    dst[r + WIDE, h, part, :] = value

    def place(src, dst, rows):
        for r in rows:
            for h in range(HALVES):
                for g in range(GROUPS):
                    dst[h, pl.ds(SUB * g * ROWS + r, SUB, stride=ROWS), :] = src[
                        r + WIDE, h, pl.ds(SUB * g, SUB), :
                    ]

    forward_coef(1)
    forward_coef(2)
    for copy in loads[first_loads:]:
        copy.wait()

    def widen(q, c):
        rows = pl.ds(pl.multiple_of(q * ROWS, ROWS), ROWS)
        for h in range(HALVES):
            pert_nat[h, rows, :] = pert_half[rows, pl.ds(h * LANES, LANES)].astype(jnp.float32)
        return c

    lax.fori_loop(0, NT * MEMBERS, widen, 0, unroll=8)

    def place_pert(r, c):
        for n in range(NT):
            for h in range(HALVES):
                for g in range(GROUPS):
                    pert_t[n, r, h, pl.ds(SUB * g, SUB), :] = pert_nat[
                        h, pl.ds((n * MEMBERS + SUB * g) * ROWS + r, SUB, stride=ROWS), :
                    ]
        return c

    lax.fori_loop(0, ROWS, place_pert, 0, unroll=2)

    four_sweeps(field, result, FORWARD, inner)
    project(mid_rows, mid_1)
    sent_m1 = to_members(mid_1, 1)
    hear()
    tell()

    for copy in coef_copies:
        copy.wait()
    forward_coef(0)
    forward_coef(3)
    for q in range(2):
        for copy in ctrl_copies[q]:
            copy.wait()
        four_sweeps(field, result, FORWARD, near_rim, only=q)
    project(edge_rows, edge_1)
    sent_e1 = to_members(edge_1, 0)
    hear()
    tell()
    adjoint_coef()

    def misfit(block, out):
        for n in range(NT):
            for h in range(HALVES):
                mis[block, HALVES * n + h] = observed(1, h, n, block == 0) * (
                    total_of(out, HALVES * n + h) - observed(0, h, n, block == 0)
                )

    wait_members(mid_1, 1)
    misfit(1, mid_1)
    pull_back(pulled, 1, mid_rows)
    pull_copies = [
        to_neighbours(half_rows(pulled, q), NEAR, ROWS - 2 * NEAR, NEAR, 6 + 2 * q)
        for q in range(2)
    ]
    hear()
    tell()
    wait_members(edge_1, 0)
    misfit(0, edge_1)
    for q in range(2):
        pull_back(pulled, 0, edge_rows, group_half[q])
        pull_copies[q] += to_neighbours(
            half_rows(pulled, q), 0, ROWS - NEAR, NEAR, 10 + 2 * q
        )

    def square(rows):
        squares = []
        for r in rows:
            for h in range(HALVES):
                for g in range(GROUPS):
                    x = grad[r + WIDE, h, pl.ds(SUB * g, SUB), :]
                    squares.append(x * x)
        while len(squares) > 1:
            squares = [a + b for a, b in zip(squares[::2], squares[1::2])]
        return squares[0]

    four_sweeps(pulled, grad, ADJOINT, inner, add=field)
    four_sweeps(grad, result, FORWARD, core)
    mid_2[m, NT * HALVES] = square(mid_rows)
    hear()
    for q in range(2):
        for copy in pull_copies[q]:
            copy.wait()
        four_sweeps(pulled, grad, ADJOINT, wide_rim, add=field, only=q)
        four_sweeps(grad, result, FORWARD, core_edge, only=q)
    project(edge_rows, edge_2)
    sent_e2 = to_members(edge_2, 2)
    mid_2[m, NT * HALVES] += square(edge_rows)
    four_sweeps(grad, result, FORWARD, core_mid)
    project(mid_rows, mid_2)
    sent_m2 = to_members(mid_2, 3)
    place(grad, grad_nat, range(ROWS))
    stores = []

    def store(src, dst, first):
        for h in range(HALVES):
            copy = pltpu.make_async_copy(
                src.at[h], dst.at[:, pl.ds(h * LANES, LANES)], out_sem.at[first + h]
            )
            copy.start()
            stores.append(copy)

    store(grad_nat, grad_out, 0)

    def weigh(block, out, total):
        for n in range(NT):
            for h in range(HALVES):
                image = total_of(out, HALVES * n + h)
                weighted = observed(1, h, n, block == 0) * image
                mis[2 + block, HALVES * n + h] = weighted
                total = total + image * weighted
        return total

    wait_members(edge_2, 2)
    observed_sum = weigh(0, edge_2, jnp.zeros((SUB, LANES), jnp.float32))
    last_copies = []
    for q in range(2):
        pull_back(pulled_2, 2, edge_rows, group_half[q])
        last_copies.append(
            to_neighbours(half_rows(pulled_2, q), 0, ROWS - NEAR, NEAR, 14 + 2 * q)
        )
    wait_members(mid_2, 3)
    observed_sum = weigh(1, mid_2, observed_sum)
    squares = total_of(mid_2, NT * HALVES)

    def fold(x):
        x = jnp.sum(x, axis=0, keepdims=True)
        return x + pltpu.roll(x, LANES // 2, 1)

    low_lane = lax.broadcasted_iota(jnp.int32, (1, LANES), 1) < LANES // 2
    scal[t] = jnp.where(low_lane, fold(squares), fold(observed_sum))

    def scalar_copy(k, slot):
        dest = lax.rem(t + k, TILE_COUNT)
        side = lax.rem(t // 2 + dest // 2, 2)
        return pltpu.make_async_remote_copy(
            src_ref=scal.at[t],
            dst_ref=scal.at[slot],
            send_sem=scal_send.at[k],
            recv_sem=scal_recv.at[k],
            device_id=(lax.rem(m + side * (MEM_COUNT // 2), MEM_COUNT), dest),
            device_id_type=MESH,
        )

    def send_scalar(k, c):
        scalar_copy(k, t).start()
        return c

    lax.fori_loop(1, TILE_COUNT, send_scalar, 0)

    pull_back(pulled_2, 3, mid_rows)
    four_sweeps(pulled_2, result, ADJOINT, inner, add=grad)
    place(result, hess_nat, mid_rows)
    for q in range(2):
        for copy in last_copies[q]:
            copy.wait()
        four_sweeps(pulled_2, result, ADJOINT, near_rim, add=grad, only=q)
    place(result, hess_nat, edge_rows)
    store(hess_nat, hess_out, HALVES)

    def wait_scalar(k, c):
        copy = scalar_copy(k, lax.rem(t + TILE_COUNT - k, TILE_COUNT))
        copy.wait_recv()
        copy.wait_send()
        return c

    lax.fori_loop(1, TILE_COUNT, wait_scalar, 0)
    sums = [scal[k] for k in range(TILE_COUNT)]
    while len(sums) > 1:
        sums = [a + b for a, b in zip(sums[::2], sums[1::2])]
    all_squares = jnp.sum(jnp.where(low_lane, sums[0], 0.0), axis=1, keepdims=True)
    all_observed = jnp.sum(jnp.where(low_lane, 0.0, sums[0]), axis=1, keepdims=True)
    step_out[...] = all_squares / (all_squares + all_observed)

    for copies in (sent_e1, sent_m1, sent_e2, sent_m2):
        for copy in copies:
            copy.wait_send()
    for copy in stores:
        copy.wait()


def hand_over(grad_in, hess_in, grad_out, hess_out, sem):
    pieces = sem.shape[1]
    copies = []
    for n, (src, dst) in enumerate(((grad_in, grad_out), (hess_in, hess_out))):
        rows = src.shape[0] // pieces
        for k in range(pieces):
            part = pl.ds(rows * k, rows)
            copies.append(pltpu.make_async_copy(src.at[part], dst.at[part], sem.at[n, k]))
    for copy in copies:
        copy.start()
    for copy in copies:
        copy.wait()


def shards(perturbations, control, innovation, obs_weight, diffusion, advection, upwind):
    f32 = jnp.float32
    cells = MEMBERS * ROWS
    width = HALVES * LANES
    any_space = pl.BlockSpec(memory_space=pl.ANY)

    def lines(count):
        return pltpu.VMEM((count, HALVES, MEMBERS, LANES), f32)

    def sums(count):
        return pltpu.VMEM((MEM_COUNT, count, SUB, LANES), f32)

    gradient, hessian, step = pl.pallas_call(
        kernel,
        out_shape=(
            jax.ShapeDtypeStruct((cells, width), f32),
            jax.ShapeDtypeStruct((cells, width), f32),
            jax.ShapeDtypeStruct((1, 1), f32),
        ),
        in_specs=[any_space] * 7,
        out_specs=(any_space, any_space, pl.BlockSpec(memory_space=pltpu.VMEM)),
        scratch_shapes=[
            pltpu.VMEM((HALVES, cells, LANES), f32),
            pltpu.VMEM((NT * cells, width), jnp.bfloat16),
            pltpu.VMEM((HALVES, NT * cells, LANES), f32),
            pltpu.VMEM((NT, ROWS, HALVES, MEMBERS, LANES), f32),
            pltpu.VMEM((2, HALVES, ROWS, LANES), f32),
            pltpu.VMEM((HALVES, ROWS, LANES), jnp.int32),
            pltpu.VMEM((2, HALVES, NT * ROWS, LANES), f32),
            pltpu.VMEM((3, HALVES, EXT, LANES), f32),
            pltpu.VMEM((10, HALVES, EXT, LANES), f32),
            *[lines(EXT)] * 8,
            sums(NT * HALVES),
            sums(NT * HALVES),
            sums(NT * HALVES),
            sums(NT * HALVES + 1),
            pltpu.VMEM((4, NT * HALVES, SUB, LANES), f32),
            pltpu.VMEM((TILE_COUNT, 1, LANES), f32),
            pltpu.VMEM((HALVES, cells, LANES), f32),
            pltpu.VMEM((HALVES, cells, LANES), f32),
            pltpu.SemaphoreType.DMA((13,)),
            pltpu.SemaphoreType.DMA((4,)),
            pltpu.SemaphoreType.DMA((18,)),
            pltpu.SemaphoreType.DMA((18,)),
            pltpu.SemaphoreType.DMA((4, MEM_COUNT)),
            pltpu.SemaphoreType.DMA((4, MEM_COUNT)),
            pltpu.SemaphoreType.DMA((TILE_COUNT,)),
            pltpu.SemaphoreType.DMA((TILE_COUNT,)),
            pltpu.SemaphoreType.REGULAR((2,)),
        ],
        compiler_params=pltpu.CompilerParams(
            collective_id=0, has_side_effects=True, vmem_limit_bytes=63 << 20
        ),
    )(
        control.reshape(cells, width),
        perturbations.reshape(NT * cells, width),
        innovation.reshape(NT * ROWS, width),
        obs_weight.reshape(NT * ROWS, width),
        diffusion,
        advection,
        upwind,
    )
    gradient, hessian = pl.pallas_call(
        hand_over,
        out_shape=(jax.ShapeDtypeStruct((cells, width), f32),) * 2,
        in_specs=[any_space] * 2,
        out_specs=(any_space, any_space),
        scratch_shapes=[pltpu.SemaphoreType.DMA((2, 4))],
    )(gradient, hessian)
    return (
        gradient.reshape(control.shape),
        hessian.reshape(control.shape),
        step.reshape(()),
    )


def solution(mesh):
    return jax.shard_map(
        shards,
        mesh=mesh,
        in_specs=(
            P(None, "mem", "tile", None),
            P("mem", "tile", None),
            P(None, "tile", None),
            P(None, "tile", None),
            P("tile", None),
            P("tile", None),
            P("tile", None),
        ),
        out_specs=(P("mem", "tile", None), P("mem", "tile", None), P()),
        check_vma=False,
    )
```

```python
import functools

import jax
import jax.numpy as jnp
from jax import lax
from jax.experimental import pallas as pl
from jax.experimental.pallas import tpu as pltpu
from jax.sharding import PartitionSpec as P

MESH = pl.DeviceIdType.MESH
SUB = 8
LANES = 128
HALVES = 2
NT = 3
ROWS = 16
MEMBERS = 32
GROUPS = MEMBERS // SUB
HALF = MEMBERS // 2
MEM_COUNT = 8
TILE_COUNT = 32
WIDE = 8
EXT = ROWS + 2 * WIDE
NEAR = 4
PLANE = 4
FORWARD = 0
ADJOINT = 5


def kernel(
    ctrl,
    pert,
    innov,
    weight,
    diff,
    adv,
    upw,
    grad_out,
    hess_out,
    step_out,
    ctrl_nat,
    pert_half,
    pert_nat,
    pert_t,
    small_in,
    upw_in,
    obs_in,
    raw,
    coef,
    field,
    level_1,
    level_2,
    level_3,
    pulled,
    grad,
    pulled_2,
    result,
    edge_1,
    mid_1,
    edge_2,
    mid_2,
    mis,
    scal,
    grad_nat,
    hess_nat,
    in_sem,
    out_sem,
    halo_send,
    halo_recv,
    red_send,
    red_recv,
    scal_send,
    scal_recv,
    known_sem,
):
    t = lax.axis_index("tile")
    m = lax.axis_index("mem")

    def tile_at(k):
        return lax.rem(t + k + TILE_COUNT, TILE_COUNT)

    barrier = pltpu.get_barrier_semaphore()
    near = [tile_at(1), tile_at(-1), tile_at(PLANE), tile_at(-PLANE)]
    near += [(t // PLANE) * PLANE + lax.rem(t + k, PLANE) for k in range(1, PLANE)]
    greeted = [(m, other) for other in near]
    greeted += [(lax.rem(m + k, MEM_COUNT), t) for k in range(1, MEM_COUNT)]
    for device in greeted:
        pl.semaphore_signal(barrier, inc=1, device_id=device, device_id_type=MESH)

    def tell():
        for n, k in enumerate((PLANE, -PLANE)):
            pl.semaphore_signal(
                known_sem.at[n], inc=1, device_id=(m, tile_at(k)), device_id_type=MESH
            )

    def hear():
        for n in range(2):
            pl.semaphore_wait(known_sem.at[n], 1)

    loads = []
    for h in range(HALVES):
        cols = pl.ds(h * LANES, LANES)
        loads.append((ctrl.at[:, cols], ctrl_nat.at[h]))
        loads.append((diff.at[:, cols], small_in.at[0, h]))
        loads.append((adv.at[:, cols], small_in.at[1, h]))
        loads.append((upw.at[:, cols], upw_in.at[h]))
    first_loads = len(loads)
    loads.append((pert, pert_half))
    for h in range(HALVES):
        cols = pl.ds(h * LANES, LANES)
        loads.append((innov.at[:, cols], obs_in.at[0, h]))
        loads.append((weight.at[:, cols], obs_in.at[1, h]))
    loads = [
        pltpu.make_async_copy(src, dst, in_sem.at[n]) for n, (src, dst) in enumerate(loads)
    ]
    for copy in loads:
        copy.start()

    lane = lax.broadcasted_iota(jnp.int32, (SUB, LANES), 1)
    sub = lax.broadcasted_iota(jnp.int32, (SUB, LANES), 0)
    low_sub = sub < SUB // 2
    at_last = lane == LANES - 1
    at_first = lane == 0

    for copy in loads[:first_loads]:
        copy.wait()

    def place_control(r, c):
        for h in range(HALVES):
            for g in range(GROUPS):
                field[r + WIDE, h, pl.ds(SUB * g, SUB), :] = ctrl_nat[
                    h, pl.ds(SUB * g * ROWS + r, SUB, stride=ROWS), :
                ]
        return c

    lax.fori_loop(0, ROWS, place_control, 0, unroll=4)
    for h in range(HALVES):
        raw[0, h, pl.ds(WIDE, ROWS), :] = small_in[0, h]
        raw[1, h, pl.ds(WIDE, ROWS), :] = small_in[1, h]
        raw[2, h, pl.ds(WIDE, ROWS), :] = jnp.where(upw_in[h] == 1, 1.0, 0.0)

    def neighbour_copies(buffer, low, high, depth, first):
        return [
            pltpu.make_async_remote_copy(
                src_ref=buffer(row + WIDE, depth),
                dst_ref=buffer(row + WIDE + shift, depth),
                send_sem=halo_send.at[first + n],
                recv_sem=halo_recv.at[first + n],
                device_id=(m, dest),
                device_id_type=MESH,
            )
            for n, (row, shift, dest) in enumerate(
                ((low, ROWS, tile_at(-1)), (high, -ROWS, tile_at(1)))
            )
        ]

    def half_copies(ref, low, high, depth, first, q):
        part = pl.ds(pl.multiple_of(HALF * q, HALF), HALF)
        return neighbour_copies(
            lambda start, count: ref.at[pl.ds(start, count), :, part, :],
            low,
            high,
            depth,
            first + 2 * q,
        )

    def start_all(copies):
        for copy in copies:
            copy.start()

    def wait_all(copies):
        for copy in copies:
            copy.wait()

    def each_half(step):
        def body(q, c):
            step(q)
            return c

        lax.fori_loop(0, 2, body, 0)

    ctrl_halo = functools.partial(half_copies, field, 0, ROWS - NEAR, NEAR, 2)
    pull_halo_mid = functools.partial(half_copies, pulled, NEAR, ROWS - 2 * NEAR, NEAR, 6)
    pull_halo_edge = functools.partial(half_copies, pulled, 0, ROWS - NEAR, NEAR, 10)
    last_halo = functools.partial(half_copies, pulled_2, 0, ROWS - NEAR, NEAR, 14)

    pl.semaphore_wait(barrier, len(greeted))

    coef_copies = neighbour_copies(
        lambda start, count: raw.at[:, :, pl.ds(start, count), :], 0, ROWS - WIDE, WIDE, 0
    )
    start_all(coef_copies)
    each_half(lambda q: start_all(ctrl_halo(q)))
    tell()

    def shifted(pair):
        lanes = lax.broadcasted_iota(jnp.int32, pair[0].shape, 1)
        right = [pltpu.roll(x, LANES - 1, 1) for x in pair]
        left = [pltpu.roll(x, 1, 1) for x in pair]
        right = [
            jnp.where(lanes == LANES - 1, right[1], right[0]),
            jnp.where(lanes == LANES - 1, 0.0, right[1]),
        ]
        left = [
            jnp.where(lanes == 0, 0.0, left[0]),
            jnp.where(lanes == 0, left[0], left[1]),
        ]
        return right, left

    top_tile = t == 0
    bottom_tile = t == TILE_COUNT - 1

    def forward_coef(block):
        rows = pl.ds(SUB * block, SUB)
        for h in range(HALVES):
            k = raw[0, h, rows, :]
            a = raw[1, h, rows, :]
            u = raw[2, h, rows, :]
            below = k + a * u
            above = k + a * (1.0 - u)
            if block == 1:
                above = jnp.where(jnp.logical_and(sub == 0, top_tile), 0.0, above)
            if block == 2:
                below = jnp.where(jnp.logical_and(sub == SUB - 1, bottom_tile), 0.0, below)
            coef[FORWARD + 0, h, rows, :] = 1.0 - 4.0 * k - a
            coef[FORWARD + 1, h, rows, :] = below
            coef[FORWARD + 2, h, rows, :] = above
            coef[FORWARD + 3, h, rows, :] = jnp.where(at_last, 0.0, k) if h else k
            coef[FORWARD + 4, h, rows, :] = k if h else jnp.where(at_first, 0.0, k)

    def adjoint_coef():
        row = lax.broadcasted_iota(jnp.int32, (EXT, LANES), 0)
        top = jnp.logical_and(row == WIDE, top_tile)
        bottom = jnp.logical_and(row == WIDE + ROWS - 1, bottom_tile)
        right, left = shifted([raw[0, h] for h in range(HALVES)])
        for h in range(HALVES):
            k = raw[0, h]
            a = raw[1, h]
            u = raw[2, h]
            below = k + a * u
            above = k + a * (1.0 - u)
            coef[ADJOINT + 0, h] = 1.0 - 4.0 * k - a
            coef[ADJOINT + 1, h] = jnp.where(bottom, 0.0, pltpu.roll(above, EXT - 1, 0))
            coef[ADJOINT + 2, h] = jnp.where(top, 0.0, pltpu.roll(below, 1, 0))
            coef[ADJOINT + 3, h] = right[h]
            coef[ADJOINT + 4, h] = left[h]

    def four_sweeps(source, target, kind, parts, add=None, half=None):
        chain = (source, level_1, level_2, level_3, target)
        together = GROUPS // 2

        def body(q, c):
            for n in range(4):
                src, dst = chain[n], chain[n + 1]
                for first, last in parts[n]:
                    for r in range(first, last):
                        f = [
                            [
                                coef[kind + i, h, pl.ds(r + WIDE, SUB, stride=0), :]
                                for h in range(HALVES)
                            ]
                            for i in range(5)
                        ]
                        for g in range(together):
                            part = pl.ds(pl.multiple_of(SUB * (together * q + g), SUB), SUB)
                            above, centre, below = [
                                [src[r + WIDE + d, h, part, :] for h in range(HALVES)]
                                for d in range(-1, 2)
                            ]
                            right = [pltpu.roll(x, LANES - 1, 1) for x in centre]
                            left = [pltpu.roll(x, 1, 1) for x in centre]
                            right = [jnp.where(at_last, right[1], right[0]), right[1]]
                            left = [left[0], jnp.where(at_first, left[0], left[1])]
                            for h in range(HALVES):
                                value = (f[0][h] * centre[h] + f[1][h] * below[h]) + (
                                    f[2][h] * above[h]
                                    + (f[3][h] * right[h] + f[4][h] * left[h])
                                )
                                if add is not None and n == 3:
                                    value = value + add[r + WIDE, h, part, :]
                                dst[r + WIDE, h, part, :] = value
            return c

        if half is not None:
            body(half, 0)
        else:
            lax.fori_loop(0, 2, body, 0)

    inner = [[(n, ROWS - n)] for n in range(1, 5)]
    near_rim = [[(n - 4, n), (ROWS - n, ROWS + 4 - n)] for n in range(1, 5)]
    wide_rim = [[(n - 8, n), (ROWS - n, ROWS + 8 - n)] for n in range(1, 5)]
    core = [[(5, 11)], [(6, 10)], [(7, 9)], []]
    core_edge = [[(-3, 5), (11, 19)], [(-2, 6), (10, 18)], [(-1, 5), (11, 17)], [(0, 4), (12, 16)]]
    core_mid = [[], [], [(5, 7), (9, 11)], [(4, 12)]]

    edge_rows = (0, 1, 2, 3, 12, 13, 14, 15)
    mid_rows = (8, 9, 10, 11, 4, 5, 6, 7)

    def project(rows, out):
        for s, r in enumerate(rows):
            for h in range(HALVES):
                value = [result[r + WIDE, h, pl.ds(SUB * g, SUB), :] for g in range(GROUPS)]
                for n in range(NT):
                    total = value[0] * pert_t[n, r, h, pl.ds(0, SUB), :]
                    for g in range(1, GROUPS):
                        total = total + value[g] * pert_t[n, r, h, pl.ds(SUB * g, SUB), :]
                    out[m, HALVES * n + h, pl.ds(s, 1), :] = jnp.sum(
                        total, axis=0, keepdims=True
                    )

    def to_members(out, first):
        copies = []
        for k in range(1, MEM_COUNT):
            copies.append(
                pltpu.make_async_remote_copy(
                    src_ref=out.at[m],
                    dst_ref=out.at[m],
                    send_sem=red_send.at[first, k],
                    recv_sem=red_recv.at[first, k],
                    device_id=(lax.rem(m + k, MEM_COUNT), t),
                    device_id_type=MESH,
                )
            )
        for copy in copies:
            copy.start()
        return copies

    def wait_members(out, first):
        for k in range(1, MEM_COUNT):
            pltpu.make_async_remote_copy(
                src_ref=out.at[m],
                dst_ref=out.at[lax.rem(m + MEM_COUNT - k, MEM_COUNT)],
                send_sem=red_send.at[first, k],
                recv_sem=red_recv.at[first, k],
                device_id=(lax.rem(m + k, MEM_COUNT), t),
                device_id_type=MESH,
            ).wait_recv()

    def total_of(out, index):
        total = [out[k, index] for k in range(MEM_COUNT)]
        while len(total) > 1:
            total = [a + b for a, b in zip(total[::2], total[1::2])]
        return total[0]

    def observed(which, h, n, edge):
        upper = obs_in[which, h, pl.ds(ROWS * n, SUB), :]
        lower = obs_in[which, h, pl.ds(ROWS * n + SUB, SUB), :]
        return jnp.where(low_sub, upper, lower) if edge else jnp.where(low_sub, lower, upper)

    def pull_back(dst, block, rows, half):
        for s, r in enumerate(rows):
            for h in range(HALVES):
                w = [
                    mis[block, HALVES * n + h, pl.ds(s, SUB, stride=0), :] for n in range(NT)
                ]
                for g in range(GROUPS // 2):
                    part = pl.ds(pl.multiple_of(HALF * half + SUB * g, SUB), SUB)
                    value = w[0] * pert_t[0, r, h, part, :]
                    for n in range(1, NT):
                        value = value + w[n] * pert_t[n, r, h, part, :]
                    dst[r + WIDE, h, part, :] = value

    def place(src, dst, rows):
        for r in rows:
            for h in range(HALVES):
                for g in range(GROUPS):
                    dst[h, pl.ds(SUB * g * ROWS + r, SUB, stride=ROWS), :] = src[
                        r + WIDE, h, pl.ds(SUB * g, SUB), :
                    ]

    forward_coef(1)
    forward_coef(2)
    for copy in loads[first_loads:]:
        copy.wait()

    def widen(q, c):
        rows = pl.ds(pl.multiple_of(q * ROWS, ROWS), ROWS)
        for h in range(HALVES):
            pert_nat[h, rows, :] = pert_half[rows, pl.ds(h * LANES, LANES)].astype(jnp.float32)
        return c

    lax.fori_loop(0, NT * MEMBERS, widen, 0, unroll=8)

    def place_pert(r, c):
        for n in range(NT):
            for h in range(HALVES):
                for g in range(GROUPS):
                    pert_t[n, r, h, pl.ds(SUB * g, SUB), :] = pert_nat[
                        h, pl.ds((n * MEMBERS + SUB * g) * ROWS + r, SUB, stride=ROWS), :
                    ]
        return c

    lax.fori_loop(0, ROWS, place_pert, 0, unroll=2)

    four_sweeps(field, result, FORWARD, inner)
    project(mid_rows, mid_1)
    sent_m1 = to_members(mid_1, 1)
    hear()
    tell()

    wait_all(coef_copies)
    forward_coef(0)
    forward_coef(3)

    def increment_rim(q):
        wait_all(ctrl_halo(q))
        four_sweeps(field, result, FORWARD, near_rim, half=q)

    each_half(increment_rim)
    project(edge_rows, edge_1)
    sent_e1 = to_members(edge_1, 0)
    hear()
    tell()
    adjoint_coef()

    def misfit(block, out):
        for n in range(NT):
            for h in range(HALVES):
                mis[block, HALVES * n + h] = observed(1, h, n, block == 0) * (
                    total_of(out, HALVES * n + h) - observed(0, h, n, block == 0)
                )

    wait_members(mid_1, 1)
    misfit(1, mid_1)

    def pull_mid(q):
        pull_back(pulled, 1, mid_rows, q)
        start_all(pull_halo_mid(q))

    each_half(pull_mid)
    hear()
    tell()
    wait_members(edge_1, 0)
    misfit(0, edge_1)

    def pull_edge(q):
        pull_back(pulled, 0, edge_rows, q)
        start_all(pull_halo_edge(q))

    each_half(pull_edge)

    def square(rows):
        squares = []
        for r in rows:
            for h in range(HALVES):
                for g in range(GROUPS):
                    x = grad[r + WIDE, h, pl.ds(SUB * g, SUB), :]
                    squares.append(x * x)
        while len(squares) > 1:
            squares = [a + b for a, b in zip(squares[::2], squares[1::2])]
        return squares[0]

    four_sweeps(pulled, grad, ADJOINT, inner, add=field)
    four_sweeps(grad, result, FORWARD, core)
    mid_2[m, NT * HALVES] = square(mid_rows)
    hear()

    def gradient_rim(q):
        wait_all(pull_halo_mid(q) + pull_halo_edge(q))
        four_sweeps(pulled, grad, ADJOINT, wide_rim, add=field, half=q)
        four_sweeps(grad, result, FORWARD, core_edge, half=q)

    each_half(gradient_rim)
    project(edge_rows, edge_2)
    sent_e2 = to_members(edge_2, 2)
    mid_2[m, NT * HALVES] += square(edge_rows)
    four_sweeps(grad, result, FORWARD, core_mid)
    project(mid_rows, mid_2)
    sent_m2 = to_members(mid_2, 3)
    place(grad, grad_nat, range(ROWS))
    stores = []

    def store(src, dst, first):
        for h in range(HALVES):
            copy = pltpu.make_async_copy(
                src.at[h], dst.at[:, pl.ds(h * LANES, LANES)], out_sem.at[first + h]
            )
            copy.start()
            stores.append(copy)

    store(grad_nat, grad_out, 0)

    def weigh(block, out, total):
        for n in range(NT):
            for h in range(HALVES):
                image = total_of(out, HALVES * n + h)
                weighted = observed(1, h, n, block == 0) * image
                mis[2 + block, HALVES * n + h] = weighted
                total = total + image * weighted
        return total

    wait_members(edge_2, 2)
    observed_sum = weigh(0, edge_2, jnp.zeros((SUB, LANES), jnp.float32))

    def last_edge(q):
        pull_back(pulled_2, 2, edge_rows, q)
        start_all(last_halo(q))

    each_half(last_edge)
    wait_members(mid_2, 3)
    observed_sum = weigh(1, mid_2, observed_sum)
    squares = total_of(mid_2, NT * HALVES)

    def fold(x):
        x = jnp.sum(x, axis=0, keepdims=True)
        return x + pltpu.roll(x, LANES // 2, 1)

    low_lane = lax.broadcasted_iota(jnp.int32, (1, LANES), 1) < LANES // 2
    scal[t] = jnp.where(low_lane, fold(squares), fold(observed_sum))

    def scalar_copy(k, slot):
        dest = lax.rem(t + k, TILE_COUNT)
        side = lax.rem(t // 2 + dest // 2, 2)
        return pltpu.make_async_remote_copy(
            src_ref=scal.at[t],
            dst_ref=scal.at[slot],
            send_sem=scal_send,
            recv_sem=scal_recv,
            device_id=(lax.rem(m + side * (MEM_COUNT // 2), MEM_COUNT), dest),
            device_id_type=MESH,
        )

    def send_scalar(k, c):
        scalar_copy(k, t).start()
        return c

    lax.fori_loop(1, TILE_COUNT, send_scalar, 0)

    each_half(lambda q: pull_back(pulled_2, 3, mid_rows, q))
    four_sweeps(pulled_2, result, ADJOINT, inner, add=grad)
    place(result, hess_nat, mid_rows)

    def hessian_rim(q):
        wait_all(last_halo(q))
        four_sweeps(pulled_2, result, ADJOINT, near_rim, add=grad, half=q)

    each_half(hessian_rim)
    place(result, hess_nat, edge_rows)
    store(hess_nat, hess_out, HALVES)

    others = scal.at[pl.ds(0, TILE_COUNT - 1)]
    pltpu.make_async_remote_copy(
        src_ref=others,
        dst_ref=others,
        send_sem=scal_send,
        recv_sem=scal_recv,
        device_id=(m, tile_at(1)),
        device_id_type=MESH,
    ).wait()
    sums = [scal[k] for k in range(TILE_COUNT)]
    while len(sums) > 1:
        sums = [a + b for a, b in zip(sums[::2], sums[1::2])]
    all_squares = jnp.sum(jnp.where(low_lane, sums[0], 0.0), axis=1, keepdims=True)
    all_observed = jnp.sum(jnp.where(low_lane, 0.0, sums[0]), axis=1, keepdims=True)
    step_out[...] = all_squares / (all_squares + all_observed)

    for copies in (sent_e1, sent_m1, sent_e2, sent_m2):
        for copy in copies:
            copy.wait_send()
    for copy in stores:
        copy.wait()


def hand_over(grad_in, hess_in, grad_out, hess_out, sem):
    copies = []
    for n, (src, dst) in enumerate(((grad_in, grad_out), (hess_in, hess_out))):
        copies.append(pltpu.make_async_copy(src, dst, sem.at[n]))
    for copy in copies:
        copy.start()
    for copy in copies:
        copy.wait()


def shards(perturbations, control, innovation, obs_weight, diffusion, advection, upwind):
    f32 = jnp.float32
    cells = MEMBERS * ROWS
    width = HALVES * LANES
    any_space = pl.BlockSpec(memory_space=pl.ANY)

    def lines(count):
        return pltpu.VMEM((count, HALVES, MEMBERS, LANES), f32)

    def sums(count):
        return pltpu.VMEM((MEM_COUNT, count, SUB, LANES), f32)

    def pin(x):
        return pltpu.with_memory_space_constraint(x, pltpu.HBM)

    gradient, hessian, step = pl.pallas_call(
        kernel,
        out_shape=(
            jax.ShapeDtypeStruct((cells, width), f32),
            jax.ShapeDtypeStruct((cells, width), f32),
            jax.ShapeDtypeStruct((1, 1), f32),
        ),
        in_specs=[any_space] * 7,
        out_specs=(any_space, any_space, pl.BlockSpec(memory_space=pltpu.VMEM)),
        scratch_shapes=[
            pltpu.VMEM((HALVES, cells, LANES), f32),
            pltpu.VMEM((NT * cells, width), jnp.bfloat16),
            pltpu.VMEM((HALVES, NT * cells, LANES), f32),
            pltpu.VMEM((NT, ROWS, HALVES, MEMBERS, LANES), f32),
            pltpu.VMEM((2, HALVES, ROWS, LANES), f32),
            pltpu.VMEM((HALVES, ROWS, LANES), jnp.int32),
            pltpu.VMEM((2, HALVES, NT * ROWS, LANES), f32),
            pltpu.VMEM((3, HALVES, EXT, LANES), f32),
            pltpu.VMEM((10, HALVES, EXT, LANES), f32),
            *[lines(EXT)] * 8,
            sums(NT * HALVES),
            sums(NT * HALVES),
            sums(NT * HALVES),
            sums(NT * HALVES + 1),
            pltpu.VMEM((4, NT * HALVES, SUB, LANES), f32),
            pltpu.VMEM((TILE_COUNT, 1, LANES), f32),
            pltpu.VMEM((HALVES, cells, LANES), f32),
            pltpu.VMEM((HALVES, cells, LANES), f32),
            pltpu.SemaphoreType.DMA((13,)),
            pltpu.SemaphoreType.DMA((4,)),
            pltpu.SemaphoreType.DMA((18,)),
            pltpu.SemaphoreType.DMA((18,)),
            pltpu.SemaphoreType.DMA((4, MEM_COUNT)),
            pltpu.SemaphoreType.DMA((4, MEM_COUNT)),
            pltpu.SemaphoreType.DMA,
            pltpu.SemaphoreType.DMA,
            pltpu.SemaphoreType.REGULAR((2,)),
        ],
        compiler_params=pltpu.CompilerParams(
            collective_id=0, has_side_effects=True, vmem_limit_bytes=20 << 20
        ),
    )(
        pin(control.reshape(cells, width)),
        pin(perturbations.reshape(NT * cells, width)),
        pin(innovation.reshape(NT * ROWS, width)),
        pin(obs_weight.reshape(NT * ROWS, width)),
        pin(diffusion),
        pin(advection),
        pin(upwind),
    )
    gradient, hessian = pl.pallas_call(
        hand_over,
        out_shape=(jax.ShapeDtypeStruct((cells, width), f32),) * 2,
        in_specs=[any_space] * 2,
        out_specs=(any_space, any_space),
        scratch_shapes=[pltpu.SemaphoreType.DMA((2,))], compiler_params=pltpu.CompilerParams(vmem_limit_bytes=1 << 20),
    )(gradient, hessian)
    return (
        gradient.reshape(control.shape),
        hessian.reshape(control.shape),
        step.reshape(()),
    )


def solution(mesh):
    return jax.shard_map(
        shards,
        mesh=mesh,
        in_specs=(
            P(None, "mem", "tile", None),
            P("mem", "tile", None),
            P(None, "tile", None),
            P(None, "tile", None),
            P("tile", None),
            P("tile", None),
            P("tile", None),
        ),
        out_specs=(P("mem", "tile", None), P("mem", "tile", None), P()),
        check_vma=False,
    )
```

```python
import functools

import jax
import jax.numpy as jnp
from jax import lax
from jax.experimental import pallas as pl
from jax.experimental.pallas import tpu as pltpu
from jax.sharding import PartitionSpec as P

MESH = pl.DeviceIdType.MESH
SUB = 8
LANES = 128
HALVES = 2
NT = 3
ROWS = 16
MEMBERS = 32
GROUPS = MEMBERS // SUB
HALF = MEMBERS // 2
MEM_COUNT = 8
TILE_COUNT = 32
WIDE = 8
EXT = ROWS + 2 * WIDE
NEAR = 4
PLANE = 4
FORWARD = 0
ADJOINT = 5


def kernel(
    ctrl,
    pert,
    innov,
    weight,
    diff,
    adv,
    upw,
    grad_out,
    hess_out,
    step_out,
    ctrl_nat,
    pert_half,
    pert_nat,
    pert_t,
    small_in,
    upw_in,
    obs_in,
    raw,
    coef,
    field,
    level_1,
    level_2,
    level_3,
    pulled,
    grad,
    pulled_2,
    result,
    edge_1,
    mid_1,
    edge_2,
    mid_2,
    mis,
    scal,
    grad_nat,
    hess_nat,
    in_sem,
    out_sem,
    halo_send,
    halo_recv,
    red_send,
    red_recv,
    scal_send,
    scal_recv,
    known_sem,
):
    t = lax.axis_index("tile")
    m = lax.axis_index("mem")

    def tile_at(k):
        return lax.rem(t + k + TILE_COUNT, TILE_COUNT)

    barrier = pltpu.get_barrier_semaphore()
    near = [tile_at(1), tile_at(-1), tile_at(PLANE), tile_at(-PLANE)]
    near += [(t // PLANE) * PLANE + lax.rem(t + k, PLANE) for k in range(1, PLANE)]
    greeted = [(m, other) for other in near]
    greeted += [(lax.rem(m + k, MEM_COUNT), t) for k in range(1, MEM_COUNT)]
    for device in greeted:
        pl.semaphore_signal(barrier, inc=1, device_id=device, device_id_type=MESH)

    def tell():
        for n, k in enumerate((PLANE, -PLANE)):
            pl.semaphore_signal(
                known_sem.at[n], inc=1, device_id=(m, tile_at(k)), device_id_type=MESH
            )

    def hear():
        for n in range(2):
            pl.semaphore_wait(known_sem.at[n], 1)

    loads = []
    for h in range(HALVES):
        cols = pl.ds(h * LANES, LANES)
        loads.append((ctrl.at[:, cols], ctrl_nat.at[h]))
        loads.append((diff.at[:, cols], small_in.at[0, h]))
        loads.append((adv.at[:, cols], small_in.at[1, h]))
        loads.append((upw.at[:, cols], upw_in.at[h]))
    first_loads = len(loads)
    loads.append((pert, pert_half))
    for h in range(HALVES):
        cols = pl.ds(h * LANES, LANES)
        loads.append((innov.at[:, cols], obs_in.at[0, h]))
        loads.append((weight.at[:, cols], obs_in.at[1, h]))
    loads = [
        pltpu.make_async_copy(src, dst, in_sem.at[n]) for n, (src, dst) in enumerate(loads)
    ]
    for copy in loads:
        copy.start()

    lane = lax.broadcasted_iota(jnp.int32, (SUB, LANES), 1)
    sub = lax.broadcasted_iota(jnp.int32, (SUB, LANES), 0)
    low_sub = sub < SUB // 2
    at_last = lane == LANES - 1
    at_first = lane == 0

    for copy in loads[:first_loads]:
        copy.wait()

    def place_control(r, c):
        for h in range(HALVES):
            for g in range(GROUPS):
                field[r + WIDE, h, pl.ds(SUB * g, SUB), :] = ctrl_nat[
                    h, pl.ds(SUB * g * ROWS + r, SUB, stride=ROWS), :
                ]
        return c

    lax.fori_loop(0, ROWS, place_control, 0, unroll=4)
    for h in range(HALVES):
        raw[0, h, pl.ds(WIDE, ROWS), :] = small_in[0, h]
        raw[1, h, pl.ds(WIDE, ROWS), :] = small_in[1, h]
        raw[2, h, pl.ds(WIDE, ROWS), :] = jnp.where(upw_in[h] == 1, 1.0, 0.0)

    def neighbour_copies(buffer, low, high, depth, first):
        return [
            pltpu.make_async_remote_copy(
                src_ref=buffer(row + WIDE, depth),
                dst_ref=buffer(row + WIDE + shift, depth),
                send_sem=halo_send.at[first + n],
                recv_sem=halo_recv.at[first + n],
                device_id=(m, dest),
                device_id_type=MESH,
            )
            for n, (row, shift, dest) in enumerate(
                ((low, ROWS, tile_at(-1)), (high, -ROWS, tile_at(1)))
            )
        ]

    def half_copies(ref, low, high, depth, first, q):
        part = pl.ds(pl.multiple_of(HALF * q, HALF), HALF)
        return neighbour_copies(
            lambda start, count: ref.at[pl.ds(start, count), :, part, :],
            low,
            high,
            depth,
            first + 2 * q,
        )

    def start_all(copies):
        for copy in copies:
            copy.start()

    def wait_all(copies):
        for copy in copies:
            copy.wait()

    def each_half(step):
        def body(q, c):
            step(q)
            return c

        lax.fori_loop(0, 2, body, 0)

    ctrl_halo = functools.partial(half_copies, field, 0, ROWS - NEAR, NEAR, 2)
    pull_halo_mid = functools.partial(half_copies, pulled, NEAR, ROWS - 2 * NEAR, NEAR, 6)
    pull_halo_edge = functools.partial(half_copies, pulled, 0, ROWS - NEAR, NEAR, 10)
    last_halo = functools.partial(half_copies, pulled_2, 0, ROWS - NEAR, NEAR, 14)

    def shifted(pair):
        lanes = lax.broadcasted_iota(jnp.int32, pair[0].shape, 1)
        right = [pltpu.roll(x, LANES - 1, 1) for x in pair]
        left = [pltpu.roll(x, 1, 1) for x in pair]
        right = [
            jnp.where(lanes == LANES - 1, right[1], right[0]),
            jnp.where(lanes == LANES - 1, 0.0, right[1]),
        ]
        left = [
            jnp.where(lanes == 0, 0.0, left[0]),
            jnp.where(lanes == 0, left[0], left[1]),
        ]
        return right, left

    top_tile = t == 0
    bottom_tile = t == TILE_COUNT - 1

    def forward_coef(block):
        rows = pl.ds(SUB * block, SUB)
        for h in range(HALVES):
            k = raw[0, h, rows, :]
            a = raw[1, h, rows, :]
            u = raw[2, h, rows, :]
            below = k + a * u
            above = k + a * (1.0 - u)
            if block == 1:
                above = jnp.where(jnp.logical_and(sub == 0, top_tile), 0.0, above)
            if block == 2:
                below = jnp.where(jnp.logical_and(sub == SUB - 1, bottom_tile), 0.0, below)
            coef[FORWARD + 0, h, rows, :] = 1.0 - 4.0 * k - a
            coef[FORWARD + 1, h, rows, :] = below
            coef[FORWARD + 2, h, rows, :] = above
            coef[FORWARD + 3, h, rows, :] = jnp.where(at_last, 0.0, k) if h else k
            coef[FORWARD + 4, h, rows, :] = k if h else jnp.where(at_first, 0.0, k)

    def adjoint_coef():
        row = lax.broadcasted_iota(jnp.int32, (EXT, LANES), 0)
        top = jnp.logical_and(row == WIDE, top_tile)
        bottom = jnp.logical_and(row == WIDE + ROWS - 1, bottom_tile)
        right, left = shifted([raw[0, h] for h in range(HALVES)])
        for h in range(HALVES):
            k = raw[0, h]
            a = raw[1, h]
            u = raw[2, h]
            below = k + a * u
            above = k + a * (1.0 - u)
            coef[ADJOINT + 0, h] = 1.0 - 4.0 * k - a
            coef[ADJOINT + 1, h] = jnp.where(bottom, 0.0, pltpu.roll(above, EXT - 1, 0))
            coef[ADJOINT + 2, h] = jnp.where(top, 0.0, pltpu.roll(below, 1, 0))
            coef[ADJOINT + 3, h] = right[h]
            coef[ADJOINT + 4, h] = left[h]

    def four_sweeps(source, target, kind, parts, add=None, half=None):
        chain = (source, level_1, level_2, level_3, target)
        together = GROUPS // 2

        def body(q, c):
            for n in range(4):
                src, dst = chain[n], chain[n + 1]
                for first, last in parts[n]:
                    for r in range(first, last):
                        f = [
                            [
                                coef[kind + i, h, pl.ds(r + WIDE, SUB, stride=0), :]
                                for h in range(HALVES)
                            ]
                            for i in range(5)
                        ]
                        for g in range(together):
                            part = pl.ds(pl.multiple_of(SUB * (together * q + g), SUB), SUB)
                            above, centre, below = [
                                [src[r + WIDE + d, h, part, :] for h in range(HALVES)]
                                for d in range(-1, 2)
                            ]
                            right = [pltpu.roll(x, LANES - 1, 1) for x in centre]
                            left = [pltpu.roll(x, 1, 1) for x in centre]
                            right = [jnp.where(at_last, right[1], right[0]), right[1]]
                            left = [left[0], jnp.where(at_first, left[0], left[1])]
                            for h in range(HALVES):
                                value = (f[0][h] * centre[h] + f[1][h] * below[h]) + (
                                    f[2][h] * above[h]
                                    + (f[3][h] * right[h] + f[4][h] * left[h])
                                )
                                if add is not None and n == 3:
                                    value = value + add[r + WIDE, h, part, :]
                                dst[r + WIDE, h, part, :] = value
            return c

        if half is not None:
            body(half, 0)
        else:
            lax.fori_loop(0, 2, body, 0)

    inner = [[(n, ROWS - n)] for n in range(1, 5)]
    near_rim = [[(n - 4, n), (ROWS - n, ROWS + 4 - n)] for n in range(1, 5)]
    wide_rim = [[(n - 8, n), (ROWS - n, ROWS + 8 - n)] for n in range(1, 5)]
    core = [[(5, 11)], [(6, 10)], [(7, 9)], []]
    core_edge = [[(-3, 5), (11, 19)], [(-2, 6), (10, 18)], [(-1, 5), (11, 17)], [(0, 4), (12, 16)]]
    core_mid = [[], [], [(5, 7), (9, 11)], [(4, 12)]]

    edge_rows = (0, 1, 2, 3, 12, 13, 14, 15)
    mid_rows = (8, 9, 10, 11, 4, 5, 6, 7)

    def project(rows, out):
        for s, r in enumerate(rows):
            for h in range(HALVES):
                value = [result[r + WIDE, h, pl.ds(SUB * g, SUB), :] for g in range(GROUPS)]
                for n in range(NT):
                    total = value[0] * pert_t[n, r, h, pl.ds(0, SUB), :]
                    for g in range(1, GROUPS):
                        total = total + value[g] * pert_t[n, r, h, pl.ds(SUB * g, SUB), :]
                    out[m, HALVES * n + h, pl.ds(s, 1), :] = jnp.sum(
                        total, axis=0, keepdims=True
                    )

    def to_members(out, first):
        copies = []
        for k in (1, 7, 2, 6, 3, 5, 4):
            copies.append(
                pltpu.make_async_remote_copy(
                    src_ref=out.at[m],
                    dst_ref=out.at[m],
                    send_sem=red_send.at[first, k],
                    recv_sem=red_recv.at[first, k],
                    device_id=(lax.rem(m + k, MEM_COUNT), t),
                    device_id_type=MESH,
                )
            )
        for copy in copies:
            copy.start()
        return copies

    def wait_members(out, first):
        for k in range(1, MEM_COUNT):
            pltpu.make_async_remote_copy(
                src_ref=out.at[m],
                dst_ref=out.at[lax.rem(m + MEM_COUNT - k, MEM_COUNT)],
                send_sem=red_send.at[first, k],
                recv_sem=red_recv.at[first, k],
                device_id=(lax.rem(m + k, MEM_COUNT), t),
                device_id_type=MESH,
            ).wait_recv()

    def total_of(out, index):
        total = [out[k, index] for k in range(MEM_COUNT)]
        while len(total) > 1:
            total = [a + b for a, b in zip(total[::2], total[1::2])]
        return total[0]

    def observed(which, h, n, edge):
        upper = obs_in[which, h, pl.ds(ROWS * n, SUB), :]
        lower = obs_in[which, h, pl.ds(ROWS * n + SUB, SUB), :]
        return jnp.where(low_sub, upper, lower) if edge else jnp.where(low_sub, lower, upper)

    def pull_back(dst, block, rows, half):
        for s, r in enumerate(rows):
            for h in range(HALVES):
                w = [
                    mis[block, HALVES * n + h, pl.ds(s, SUB, stride=0), :] for n in range(NT)
                ]
                for g in range(GROUPS // 2):
                    part = pl.ds(pl.multiple_of(HALF * half + SUB * g, SUB), SUB)
                    value = w[0] * pert_t[0, r, h, part, :]
                    for n in range(1, NT):
                        value = value + w[n] * pert_t[n, r, h, part, :]
                    dst[r + WIDE, h, part, :] = value

    def place(src, dst, rows):
        for r in rows:
            for h in range(HALVES):
                for g in range(GROUPS):
                    dst[h, pl.ds(SUB * g * ROWS + r, SUB, stride=ROWS), :] = src[
                        r + WIDE, h, pl.ds(SUB * g, SUB), :
                    ]

    forward_coef(1)
    forward_coef(2)
    for copy in loads[first_loads:]:
        copy.wait()

    def widen(q, c):
        rows = pl.ds(pl.multiple_of(q * ROWS, ROWS), ROWS)
        for h in range(HALVES):
            pert_nat[h, rows, :] = pert_half[rows, pl.ds(h * LANES, LANES)].astype(jnp.float32)
        return c

    lax.fori_loop(0, NT * MEMBERS, widen, 0, unroll=8)

    def place_pert(r, c):
        for n in range(NT):
            for h in range(HALVES):
                for g in range(GROUPS):
                    pert_t[n, r, h, pl.ds(SUB * g, SUB), :] = pert_nat[
                        h, pl.ds((n * MEMBERS + SUB * g) * ROWS + r, SUB, stride=ROWS), :
                    ]
        return c

    lax.fori_loop(0, ROWS, place_pert, 0, unroll=2)

    four_sweeps(field, result, FORWARD, inner)
    project(mid_rows, mid_1)

    pl.semaphore_wait(barrier, len(greeted))

    coef_copies = neighbour_copies(
        lambda start, count: raw.at[:, :, pl.ds(start, count), :], 0, ROWS - WIDE, WIDE, 0
    )
    start_all(coef_copies)
    each_half(lambda q: start_all(ctrl_halo(q)))
    tell()
    sent_m1 = to_members(mid_1, 1)
    hear()
    tell()

    wait_all(coef_copies)
    forward_coef(0)
    forward_coef(3)

    def increment_rim(q):
        wait_all(ctrl_halo(q))
        four_sweeps(field, result, FORWARD, near_rim, half=q)

    each_half(increment_rim)
    project(edge_rows, edge_1)
    sent_e1 = to_members(edge_1, 0)
    hear()
    tell()
    adjoint_coef()

    def misfit(block, out):
        for n in range(NT):
            for h in range(HALVES):
                mis[block, HALVES * n + h] = observed(1, h, n, block == 0) * (
                    total_of(out, HALVES * n + h) - observed(0, h, n, block == 0)
                )

    wait_members(mid_1, 1)
    misfit(1, mid_1)

    def pull_mid(q):
        pull_back(pulled, 1, mid_rows, q)
        start_all(pull_halo_mid(q))

    each_half(pull_mid)
    hear()
    tell()
    wait_members(edge_1, 0)
    misfit(0, edge_1)

    def pull_edge(q):
        pull_back(pulled, 0, edge_rows, q)
        start_all(pull_halo_edge(q))

    each_half(pull_edge)

    def square(rows):
        squares = []
        for r in rows:
            for h in range(HALVES):
                for g in range(GROUPS):
                    x = grad[r + WIDE, h, pl.ds(SUB * g, SUB), :]
                    squares.append(x * x)
        while len(squares) > 1:
            squares = [a + b for a, b in zip(squares[::2], squares[1::2])]
        return squares[0]

    four_sweeps(pulled, grad, ADJOINT, inner, add=field)
    four_sweeps(grad, result, FORWARD, core)
    mid_2[m, NT * HALVES] = square(mid_rows)
    hear()

    def gradient_rim(q):
        wait_all(pull_halo_mid(q) + pull_halo_edge(q))
        four_sweeps(pulled, grad, ADJOINT, wide_rim, add=field, half=q)
        four_sweeps(grad, result, FORWARD, core_edge, half=q)

    each_half(gradient_rim)
    project(edge_rows, edge_2)
    sent_e2 = to_members(edge_2, 2)
    mid_2[m, NT * HALVES] += square(edge_rows)
    four_sweeps(grad, result, FORWARD, core_mid)
    project(mid_rows, mid_2)
    sent_m2 = to_members(mid_2, 3)
    place(grad, grad_nat, range(ROWS))
    stores = []

    def store(src, dst, first):
        for h in range(HALVES):
            copy = pltpu.make_async_copy(
                src.at[h], dst.at[:, pl.ds(h * LANES, LANES)], out_sem.at[first + h]
            )
            copy.start()
            stores.append(copy)

    store(grad_nat, grad_out, 0)

    def weigh(block, out, total):
        for n in range(NT):
            for h in range(HALVES):
                image = total_of(out, HALVES * n + h)
                weighted = observed(1, h, n, block == 0) * image
                mis[2 + block, HALVES * n + h] = weighted
                total = total + image * weighted
        return total

    wait_members(edge_2, 2)
    observed_sum = weigh(0, edge_2, jnp.zeros((SUB, LANES), jnp.float32))

    def last_edge(q):
        pull_back(pulled_2, 2, edge_rows, q)
        start_all(last_halo(q))

    each_half(last_edge)
    wait_members(mid_2, 3)
    observed_sum = weigh(1, mid_2, observed_sum)
    squares = total_of(mid_2, NT * HALVES)

    def fold(x):
        x = jnp.sum(x, axis=0, keepdims=True)
        return x + pltpu.roll(x, LANES // 2, 1)

    low_lane = lax.broadcasted_iota(jnp.int32, (1, LANES), 1) < LANES // 2
    scal[t] = jnp.where(low_lane, fold(squares), fold(observed_sum))

    def scalar_copy(k, slot):
        dest = lax.rem(t + k, TILE_COUNT)
        side = lax.rem(t // 2 + dest // 2, 2)
        return pltpu.make_async_remote_copy(
            src_ref=scal.at[t],
            dst_ref=scal.at[slot],
            send_sem=scal_send,
            recv_sem=scal_recv,
            device_id=(lax.rem(m + side * (MEM_COUNT // 2), MEM_COUNT), dest),
            device_id_type=MESH,
        )

    def send_scalar(k, c):
        scalar_copy(k, t).start()
        return c

    lax.fori_loop(1, TILE_COUNT, send_scalar, 0)

    each_half(lambda q: pull_back(pulled_2, 3, mid_rows, q))
    four_sweeps(pulled_2, result, ADJOINT, inner, add=grad)
    place(result, hess_nat, mid_rows)

    def hessian_rim(q):
        wait_all(last_halo(q))
        four_sweeps(pulled_2, result, ADJOINT, near_rim, add=grad, half=q)

    each_half(hessian_rim)
    place(result, hess_nat, edge_rows)
    store(hess_nat, hess_out, HALVES)

    others = scal.at[pl.ds(0, TILE_COUNT - 1)]
    pltpu.make_async_remote_copy(
        src_ref=others,
        dst_ref=others,
        send_sem=scal_send,
        recv_sem=scal_recv,
        device_id=(m, tile_at(1)),
        device_id_type=MESH,
    ).wait()
    sums = [scal[k] for k in range(TILE_COUNT)]
    while len(sums) > 1:
        sums = [a + b for a, b in zip(sums[::2], sums[1::2])]
    all_squares = jnp.sum(jnp.where(low_lane, sums[0], 0.0), axis=1, keepdims=True)
    all_observed = jnp.sum(jnp.where(low_lane, 0.0, sums[0]), axis=1, keepdims=True)
    step_out[...] = all_squares / (all_squares + all_observed)

    for copies in (sent_e1, sent_m1, sent_e2, sent_m2):
        for copy in copies:
            copy.wait_send()
    for copy in stores:
        copy.wait()


def hand_over(grad_in, hess_in, grad_out, hess_out, sem):
    copies = []
    for n, (src, dst) in enumerate(((grad_in, grad_out), (hess_in, hess_out))):
        copies.append(pltpu.make_async_copy(src, dst, sem.at[n]))
    for copy in copies:
        copy.start()
    for copy in copies:
        copy.wait()


def shards(perturbations, control, innovation, obs_weight, diffusion, advection, upwind):
    f32 = jnp.float32
    cells = MEMBERS * ROWS
    width = HALVES * LANES
    any_space = pl.BlockSpec(memory_space=pl.ANY)

    def lines(count):
        return pltpu.VMEM((count, HALVES, MEMBERS, LANES), f32)

    def sums(count):
        return pltpu.VMEM((MEM_COUNT, count, SUB, LANES), f32)

    def pin(x):
        return pltpu.with_memory_space_constraint(x, pltpu.HBM)

    gradient, hessian, step = pl.pallas_call(
        kernel,
        out_shape=(
            jax.ShapeDtypeStruct((cells, width), f32),
            jax.ShapeDtypeStruct((cells, width), f32),
            jax.ShapeDtypeStruct((1, 1), f32),
        ),
        in_specs=[any_space] * 7,
        out_specs=(any_space, any_space, pl.BlockSpec(memory_space=pltpu.VMEM)),
        scratch_shapes=[
            pltpu.VMEM((HALVES, cells, LANES), f32),
            pltpu.VMEM((NT * cells, width), jnp.bfloat16),
            pltpu.VMEM((HALVES, NT * cells, LANES), f32),
            pltpu.VMEM((NT, ROWS, HALVES, MEMBERS, LANES), f32),
            pltpu.VMEM((2, HALVES, ROWS, LANES), f32),
            pltpu.VMEM((HALVES, ROWS, LANES), jnp.int32),
            pltpu.VMEM((2, HALVES, NT * ROWS, LANES), f32),
            pltpu.VMEM((3, HALVES, EXT, LANES), f32),
            pltpu.VMEM((10, HALVES, EXT, LANES), f32),
            *[lines(EXT)] * 8,
            sums(NT * HALVES),
            sums(NT * HALVES),
            sums(NT * HALVES),
            sums(NT * HALVES + 1),
            pltpu.VMEM((4, NT * HALVES, SUB, LANES), f32),
            pltpu.VMEM((TILE_COUNT, 1, LANES), f32),
            pltpu.VMEM((HALVES, cells, LANES), f32),
            pltpu.VMEM((HALVES, cells, LANES), f32),
            pltpu.SemaphoreType.DMA((13,)),
            pltpu.SemaphoreType.DMA((4,)),
            pltpu.SemaphoreType.DMA((18,)),
            pltpu.SemaphoreType.DMA((18,)),
            pltpu.SemaphoreType.DMA((4, MEM_COUNT)),
            pltpu.SemaphoreType.DMA((4, MEM_COUNT)),
            pltpu.SemaphoreType.DMA,
            pltpu.SemaphoreType.DMA,
            pltpu.SemaphoreType.REGULAR((2,)),
        ],
        compiler_params=pltpu.CompilerParams(
            collective_id=0, has_side_effects=True, vmem_limit_bytes=20 << 20
        ),
    )(
        pin(control.reshape(cells, width)),
        pin(perturbations.reshape(NT * cells, width)),
        pin(innovation.reshape(NT * ROWS, width)),
        pin(obs_weight.reshape(NT * ROWS, width)),
        pin(diffusion),
        pin(advection),
        pin(upwind),
    )
    gradient, hessian = pl.pallas_call(
        hand_over,
        out_shape=(jax.ShapeDtypeStruct((cells, width), f32),) * 2,
        in_specs=[any_space] * 2,
        out_specs=(any_space, any_space),
        scratch_shapes=[pltpu.SemaphoreType.DMA((2,))], compiler_params=pltpu.CompilerParams(vmem_limit_bytes=1 << 20),
    )(gradient, hessian)
    return (
        gradient.reshape(control.shape),
        hessian.reshape(control.shape),
        step.reshape(()),
    )


def solution(mesh):
    return jax.shard_map(
        shards,
        mesh=mesh,
        in_specs=(
            P(None, "mem", "tile", None),
            P("mem", "tile", None),
            P(None, "tile", None),
            P(None, "tile", None),
            P("tile", None),
            P("tile", None),
            P("tile", None),
        ),
        out_specs=(P("mem", "tile", None), P("mem", "tile", None), P()),
        check_vma=False,
    )
```

```python
import functools

import jax
import jax.numpy as jnp
from jax import lax
from jax.experimental import pallas as pl
from jax.experimental.pallas import tpu as pltpu
from jax.sharding import PartitionSpec as P

MESH = pl.DeviceIdType.MESH
SUB = 8
LANES = 128
HALVES = 2
NT = 3
ROWS = 16
MEMBERS = 32
GROUPS = MEMBERS // SUB
HALF = MEMBERS // 2
MEM_COUNT = 8
TILE_COUNT = 32
WIDE = 8
EXT = ROWS + 2 * WIDE
NEAR = 4
PLANE = 4
FORWARD = 0
ADJOINT = 5


def kernel(
    ctrl,
    pert,
    innov,
    weight,
    diff,
    adv,
    upw,
    grad_out,
    hess_out,
    step_out,
    ctrl_nat,
    pert_half,
    pert_nat,
    pert_t,
    small_in,
    upw_in,
    obs_in,
    raw,
    coef,
    field,
    level_1,
    level_2,
    level_3,
    pulled,
    grad,
    pulled_2,
    result,
    edge_1,
    mid_1,
    edge_2,
    mid_2,
    mis,
    scal,
    grad_nat,
    hess_nat,
    in_sem,
    out_sem,
    halo_send,
    halo_recv,
    red_send,
    red_recv,
    scal_send,
    scal_recv,
    known_sem,
):
    t = lax.axis_index("tile")
    m = lax.axis_index("mem")

    def tile_at(k):
        return lax.rem(t + k + TILE_COUNT, TILE_COUNT)

    barrier = pltpu.get_barrier_semaphore()
    near = [tile_at(1), tile_at(-1), tile_at(PLANE), tile_at(-PLANE)]
    near += [(t // PLANE) * PLANE + lax.rem(t + k, PLANE) for k in range(1, PLANE)]
    greeted = [(m, other) for other in near]
    greeted += [(lax.rem(m + k, MEM_COUNT), t) for k in range(1, MEM_COUNT)]
    for device in greeted:
        pl.semaphore_signal(barrier, inc=1, device_id=device, device_id_type=MESH)

    def tell():
        for n, k in enumerate((PLANE, -PLANE)):
            pl.semaphore_signal(
                known_sem.at[n], inc=1, device_id=(m, tile_at(k)), device_id_type=MESH
            )

    def hear():
        for n in range(2):
            pl.semaphore_wait(known_sem.at[n], 1)

    loads = []
    for h in range(HALVES):
        cols = pl.ds(h * LANES, LANES)
        loads.append((ctrl.at[:, cols], ctrl_nat.at[h]))
        loads.append((diff.at[:, cols], small_in.at[0, h]))
        loads.append((adv.at[:, cols], small_in.at[1, h]))
        loads.append((upw.at[:, cols], upw_in.at[h]))
    first_loads = len(loads)
    loads.append((pert, pert_half))
    for h in range(HALVES):
        cols = pl.ds(h * LANES, LANES)
        loads.append((innov.at[:, cols], obs_in.at[0, h]))
        loads.append((weight.at[:, cols], obs_in.at[1, h]))
    loads = [
        pltpu.make_async_copy(src, dst, in_sem.at[n]) for n, (src, dst) in enumerate(loads)
    ]
    for copy in loads:
        copy.start()

    lane = lax.broadcasted_iota(jnp.int32, (SUB, LANES), 1)
    sub = lax.broadcasted_iota(jnp.int32, (SUB, LANES), 0)
    low_sub = sub < SUB // 2
    at_last = lane == LANES - 1
    at_first = lane == 0

    for copy in loads[:first_loads]:
        copy.wait()

    def place_control(r, c):
        for h in range(HALVES):
            for g in range(GROUPS):
                field[r + WIDE, h, pl.ds(SUB * g, SUB), :] = ctrl_nat[
                    h, pl.ds(SUB * g * ROWS + r, SUB, stride=ROWS), :
                ]
        return c

    lax.fori_loop(0, ROWS, place_control, 0, unroll=4)
    for h in range(HALVES):
        raw[0, h, pl.ds(WIDE, ROWS), :] = small_in[0, h]
        raw[1, h, pl.ds(WIDE, ROWS), :] = small_in[1, h]
        raw[2, h, pl.ds(WIDE, ROWS), :] = jnp.where(upw_in[h] == 1, 1.0, 0.0)

    def neighbour_copies(buffer, low, high, depth, first):
        return [
            pltpu.make_async_remote_copy(
                src_ref=buffer(row + WIDE, depth),
                dst_ref=buffer(row + WIDE + shift, depth),
                send_sem=halo_send.at[first + n],
                recv_sem=halo_recv.at[first + n],
                device_id=(m, dest),
                device_id_type=MESH,
            )
            for n, (row, shift, dest) in enumerate(
                ((low, ROWS, tile_at(-1)), (high, -ROWS, tile_at(1)))
            )
        ]

    def half_copies(ref, low, high, depth, first, q):
        part = pl.ds(pl.multiple_of(HALF * q, HALF), HALF)
        return neighbour_copies(
            lambda start, count: ref.at[pl.ds(start, count), :, part, :],
            low,
            high,
            depth,
            first + 2 * q,
        )

    def start_all(copies):
        for copy in copies:
            copy.start()

    def wait_all(copies):
        for copy in copies:
            copy.wait()

    def each_half(step):
        def body(q, c):
            step(q)
            return c

        lax.fori_loop(0, 2, body, 0)

    ctrl_halo = functools.partial(half_copies, field, 0, ROWS - NEAR, NEAR, 2)
    pull_halo_mid = functools.partial(half_copies, pulled, NEAR, ROWS - 2 * NEAR, NEAR, 6)
    pull_halo_edge = functools.partial(half_copies, pulled, 0, ROWS - NEAR, NEAR, 10)
    last_halo = functools.partial(half_copies, pulled_2, 0, ROWS - NEAR, NEAR, 14)

    def shifted(pair):
        lanes = lax.broadcasted_iota(jnp.int32, pair[0].shape, 1)
        right = [pltpu.roll(x, LANES - 1, 1) for x in pair]
        left = [pltpu.roll(x, 1, 1) for x in pair]
        right = [
            jnp.where(lanes == LANES - 1, right[1], right[0]),
            jnp.where(lanes == LANES - 1, 0.0, right[1]),
        ]
        left = [
            jnp.where(lanes == 0, 0.0, left[0]),
            jnp.where(lanes == 0, left[0], left[1]),
        ]
        return right, left

    top_tile = t == 0
    bottom_tile = t == TILE_COUNT - 1

    def forward_coef(block):
        rows = pl.ds(SUB * block, SUB)
        for h in range(HALVES):
            k = raw[0, h, rows, :]
            a = raw[1, h, rows, :]
            u = raw[2, h, rows, :]
            below = k + a * u
            above = k + a * (1.0 - u)
            if block == 1:
                above = jnp.where(jnp.logical_and(sub == 0, top_tile), 0.0, above)
            if block == 2:
                below = jnp.where(jnp.logical_and(sub == SUB - 1, bottom_tile), 0.0, below)
            coef[FORWARD + 0, h, rows, :] = 1.0 - 4.0 * k - a
            coef[FORWARD + 1, h, rows, :] = below
            coef[FORWARD + 2, h, rows, :] = above
            coef[FORWARD + 3, h, rows, :] = jnp.where(at_last, 0.0, k) if h else k
            coef[FORWARD + 4, h, rows, :] = k if h else jnp.where(at_first, 0.0, k)

    def adjoint_coef():
        row = lax.broadcasted_iota(jnp.int32, (EXT, LANES), 0)
        top = jnp.logical_and(row == WIDE, top_tile)
        bottom = jnp.logical_and(row == WIDE + ROWS - 1, bottom_tile)
        right, left = shifted([raw[0, h] for h in range(HALVES)])
        for h in range(HALVES):
            k = raw[0, h]
            a = raw[1, h]
            u = raw[2, h]
            below = k + a * u
            above = k + a * (1.0 - u)
            coef[ADJOINT + 0, h] = 1.0 - 4.0 * k - a
            coef[ADJOINT + 1, h] = jnp.where(bottom, 0.0, pltpu.roll(above, EXT - 1, 0))
            coef[ADJOINT + 2, h] = jnp.where(top, 0.0, pltpu.roll(below, 1, 0))
            coef[ADJOINT + 3, h] = right[h]
            coef[ADJOINT + 4, h] = left[h]

    def four_sweeps(source, target, kind, parts, add=None, half=None):
        chain = (source, level_1, level_2, level_3, target)
        together = GROUPS // 2

        def body(q, c):
            for n in range(4):
                src, dst = chain[n], chain[n + 1]
                for first, last in parts[n]:
                    for r in range(first, last):
                        f = [
                            [
                                coef[kind + i, h, pl.ds(r + WIDE, SUB, stride=0), :]
                                for h in range(HALVES)
                            ]
                            for i in range(5)
                        ]
                        for g in range(together):
                            part = pl.ds(pl.multiple_of(SUB * (together * q + g), SUB), SUB)
                            above, centre, below = [
                                [src[r + WIDE + d, h, part, :] for h in range(HALVES)]
                                for d in range(-1, 2)
                            ]
                            right = [pltpu.roll(x, LANES - 1, 1) for x in centre]
                            left = [pltpu.roll(x, 1, 1) for x in centre]
                            right = [jnp.where(at_last, right[1], right[0]), right[1]]
                            left = [left[0], jnp.where(at_first, left[0], left[1])]
                            for h in range(HALVES):
                                value = (f[0][h] * centre[h] + f[1][h] * below[h]) + (
                                    f[2][h] * above[h]
                                    + (f[3][h] * right[h] + f[4][h] * left[h])
                                )
                                if add is not None and n == 3:
                                    value = value + add[r + WIDE, h, part, :]
                                dst[r + WIDE, h, part, :] = value
            return c

        if half is not None:
            body(half, 0)
        else:
            lax.fori_loop(0, 2, body, 0)

    inner = [[(n, ROWS - n)] for n in range(1, 5)]
    near_rim = [[(n - 4, n), (ROWS - n, ROWS + 4 - n)] for n in range(1, 5)]
    wide_rim = [[(n - 8, n), (ROWS - n, ROWS + 8 - n)] for n in range(1, 5)]
    core = [[(5, 11)], [(6, 10)], [(7, 9)], []]
    core_edge = [[(-3, 5), (11, 19)], [(-2, 6), (10, 18)], [(-1, 5), (11, 17)], [(0, 4), (12, 16)]]
    core_mid = [[], [], [(5, 7), (9, 11)], [(4, 12)]]

    edge_rows = (0, 1, 2, 3, 12, 13, 14, 15)
    mid_rows = (8, 9, 10, 11, 4, 5, 6, 7)

    def project(rows, out):
        for s, r in enumerate(rows):
            for h in range(HALVES):
                value = [result[r + WIDE, h, pl.ds(SUB * g, SUB), :] for g in range(GROUPS)]
                for n in range(NT):
                    total = value[0] * pert_t[n, r, h, pl.ds(0, SUB), :]
                    for g in range(1, GROUPS):
                        total = total + value[g] * pert_t[n, r, h, pl.ds(SUB * g, SUB), :]
                    out[m, HALVES * n + h, pl.ds(s, 1), :] = jnp.sum(
                        total, axis=0, keepdims=True
                    )

    def to_members(out, first):
        copies = []
        for k in (1, 7, 2, 6, 3, 5, 4):
            copies.append(
                pltpu.make_async_remote_copy(
                    src_ref=out.at[m],
                    dst_ref=out.at[m],
                    send_sem=red_send.at[first, k],
                    recv_sem=red_recv.at[first, k],
                    device_id=(lax.rem(m + k, MEM_COUNT), t),
                    device_id_type=MESH,
                )
            )
        for copy in copies:
            copy.start()
        return copies

    def wait_members(out, first):
        for k in range(1, MEM_COUNT):
            pltpu.make_async_remote_copy(
                src_ref=out.at[m],
                dst_ref=out.at[lax.rem(m + MEM_COUNT - k, MEM_COUNT)],
                send_sem=red_send.at[first, k],
                recv_sem=red_recv.at[first, k],
                device_id=(lax.rem(m + k, MEM_COUNT), t),
                device_id_type=MESH,
            ).wait_recv()

    def total_of(out, index):
        total = [out[k, index] for k in range(MEM_COUNT)]
        while len(total) > 1:
            total = [a + b for a, b in zip(total[::2], total[1::2])]
        return total[0]

    def observed(which, h, n, edge):
        upper = obs_in[which, h, pl.ds(ROWS * n, SUB), :]
        lower = obs_in[which, h, pl.ds(ROWS * n + SUB, SUB), :]
        return jnp.where(low_sub, upper, lower) if edge else jnp.where(low_sub, lower, upper)

    def pull_back(dst, block, rows, half):
        for s, r in enumerate(rows):
            for h in range(HALVES):
                w = [
                    mis[block, HALVES * n + h, pl.ds(s, SUB, stride=0), :] for n in range(NT)
                ]
                for g in range(GROUPS // 2):
                    part = pl.ds(pl.multiple_of(HALF * half + SUB * g, SUB), SUB)
                    value = w[0] * pert_t[0, r, h, part, :]
                    for n in range(1, NT):
                        value = value + w[n] * pert_t[n, r, h, part, :]
                    dst[r + WIDE, h, part, :] = value

    def place(src, dst, rows):
        for r in rows:
            for h in range(HALVES):
                for g in range(GROUPS):
                    dst[h, pl.ds(SUB * g * ROWS + r, SUB, stride=ROWS), :] = src[
                        r + WIDE, h, pl.ds(SUB * g, SUB), :
                    ]

    forward_coef(1)
    forward_coef(2)
    for copy in loads[first_loads:]:
        copy.wait()

    def widen(q, c):
        rows = pl.ds(pl.multiple_of(q * ROWS, ROWS), ROWS)
        for h in range(HALVES):
            pert_nat[h, rows, :] = pert_half[rows, pl.ds(h * LANES, LANES)].astype(jnp.float32)
        return c

    lax.fori_loop(0, NT * MEMBERS, widen, 0, unroll=8)

    def place_pert(r, c):
        for n in range(NT):
            for h in range(HALVES):
                for g in range(GROUPS):
                    pert_t[n, r, h, pl.ds(SUB * g, SUB), :] = pert_nat[
                        h, pl.ds((n * MEMBERS + SUB * g) * ROWS + r, SUB, stride=ROWS), :
                    ]
        return c

    lax.fori_loop(0, ROWS, place_pert, 0, unroll=2)

    four_sweeps(field, result, FORWARD, inner)
    project(mid_rows, mid_1)

    pl.semaphore_wait(barrier, len(greeted))

    coef_copies = neighbour_copies(
        lambda start, count: raw.at[:, :, pl.ds(start, count), :], 0, ROWS - WIDE, WIDE, 0
    )
    start_all(coef_copies)
    each_half(lambda q: start_all(ctrl_halo(q)))
    tell()
    sent_m1 = to_members(mid_1, 1)
    hear()
    tell()

    wait_all(coef_copies)
    forward_coef(0)
    forward_coef(3)

    def increment_rim(q):
        wait_all(ctrl_halo(q))
        four_sweeps(field, result, FORWARD, near_rim, half=q)

    each_half(increment_rim)
    project(edge_rows, edge_1)
    sent_e1 = to_members(edge_1, 0)
    hear()
    tell()
    adjoint_coef()

    def misfit(block, out):
        for n in range(NT):
            for h in range(HALVES):
                mis[block, HALVES * n + h] = observed(1, h, n, block == 0) * (
                    total_of(out, HALVES * n + h) - observed(0, h, n, block == 0)
                )

    wait_members(mid_1, 1)
    misfit(1, mid_1)

    def pull_mid(q):
        pull_back(pulled, 1, mid_rows, q)
        start_all(pull_halo_mid(q))

    each_half(pull_mid)
    hear()
    tell()
    wait_members(edge_1, 0)
    misfit(0, edge_1)

    def pull_edge(q):
        pull_back(pulled, 0, edge_rows, q)
        start_all(pull_halo_edge(q))

    each_half(pull_edge)

    def square(rows):
        squares = []
        for r in rows:
            for h in range(HALVES):
                for g in range(GROUPS):
                    x = grad[r + WIDE, h, pl.ds(SUB * g, SUB), :]
                    squares.append(x * x)
        while len(squares) > 1:
            squares = [a + b for a, b in zip(squares[::2], squares[1::2])]
        return squares[0]

    four_sweeps(pulled, grad, ADJOINT, inner, add=field)
    four_sweeps(grad, result, FORWARD, core)
    mid_2[m, NT * HALVES] = square(mid_rows)
    hear()

    def gradient_rim(q):
        wait_all(pull_halo_mid(q) + pull_halo_edge(q))
        four_sweeps(pulled, grad, ADJOINT, wide_rim, add=field, half=q)
        four_sweeps(grad, result, FORWARD, core_edge, half=q)

    each_half(gradient_rim)
    project(edge_rows, edge_2)
    sent_e2 = to_members(edge_2, 2)
    mid_2[m, NT * HALVES] += square(edge_rows)
    four_sweeps(grad, result, FORWARD, core_mid)
    project(mid_rows, mid_2)
    sent_m2 = to_members(mid_2, 3)
    place(grad, grad_nat, range(ROWS))
    stores = []

    def store(src, dst, first):
        for h in range(HALVES):
            copy = pltpu.make_async_copy(
                src.at[h], dst.at[:, pl.ds(h * LANES, LANES)], out_sem.at[first + h]
            )
            copy.start()
            stores.append(copy)

    store(grad_nat, grad_out, 0)

    def weigh(block, out, total):
        for n in range(NT):
            for h in range(HALVES):
                image = total_of(out, HALVES * n + h)
                weighted = observed(1, h, n, block == 0) * image
                mis[2 + block, HALVES * n + h] = weighted
                total = total + image * weighted
        return total

    wait_members(edge_2, 2)
    observed_sum = weigh(0, edge_2, jnp.zeros((SUB, LANES), jnp.float32))

    def last_edge(q):
        pull_back(pulled_2, 2, edge_rows, q)
        start_all(last_halo(q))

    each_half(last_edge)
    wait_members(mid_2, 3)
    observed_sum = weigh(1, mid_2, observed_sum)
    squares = total_of(mid_2, NT * HALVES)

    def fold(x):
        x = jnp.sum(x, axis=0, keepdims=True)
        return x + pltpu.roll(x, LANES // 2, 1)

    low_lane = lax.broadcasted_iota(jnp.int32, (1, LANES), 1) < LANES // 2
    scal[t] = jnp.where(low_lane, fold(squares), fold(observed_sum))

    def scalar_copy(k, slot):
        dest = lax.rem(t + k, TILE_COUNT)
        side = lax.rem(t // 2 + dest // 2, 2)
        return pltpu.make_async_remote_copy(
            src_ref=scal.at[t],
            dst_ref=scal.at[slot],
            send_sem=scal_send,
            recv_sem=scal_recv,
            device_id=(lax.rem(m + side * (MEM_COUNT // 2), MEM_COUNT), dest),
            device_id_type=MESH,
        )

    def send_scalar(k, c):
        scalar_copy(k, t).start()
        return c

    lax.fori_loop(1, TILE_COUNT, send_scalar, 0)

    each_half(lambda q: pull_back(pulled_2, 3, mid_rows, q))
    four_sweeps(pulled_2, result, ADJOINT, inner, add=grad)
    place(result, hess_nat, mid_rows)

    for copies in (sent_e1, sent_m1, sent_e2, sent_m2):
        for copy in copies:
            copy.wait_send()

    def hessian_rim(q):
        wait_all(last_halo(q))
        four_sweeps(pulled_2, result, ADJOINT, near_rim, add=grad, half=q)

    each_half(hessian_rim)
    place(result, hess_nat, edge_rows)
    store(hess_nat, hess_out, HALVES)

    for copy in stores:
        copy.wait()
    others = scal.at[pl.ds(0, TILE_COUNT - 1)]
    pltpu.make_async_remote_copy(
        src_ref=others,
        dst_ref=others,
        send_sem=scal_send,
        recv_sem=scal_recv,
        device_id=(m, tile_at(1)),
        device_id_type=MESH,
    ).wait()
    sums = [scal[k] for k in range(TILE_COUNT)]
    while len(sums) > 1:
        sums = [a + b for a, b in zip(sums[::2], sums[1::2])]
    all_squares = jnp.sum(jnp.where(low_lane, sums[0], 0.0), axis=1, keepdims=True)
    all_observed = jnp.sum(jnp.where(low_lane, 0.0, sums[0]), axis=1, keepdims=True)
    step_out[...] = all_squares / (all_squares + all_observed)


def hand_over(grad_in, hess_in, grad_out, hess_out, sem):
    copies = []
    for n, (src, dst) in enumerate(((grad_in, grad_out), (hess_in, hess_out))):
        copies.append(pltpu.make_async_copy(src, dst, sem.at[n]))
    for copy in copies:
        copy.start()
    for copy in copies:
        copy.wait()


def shards(perturbations, control, innovation, obs_weight, diffusion, advection, upwind):
    f32 = jnp.float32
    cells = MEMBERS * ROWS
    width = HALVES * LANES
    any_space = pl.BlockSpec(memory_space=pl.ANY)

    def lines(count):
        return pltpu.VMEM((count, HALVES, MEMBERS, LANES), f32)

    def sums(count):
        return pltpu.VMEM((MEM_COUNT, count, SUB, LANES), f32)

    def pin(x):
        return pltpu.with_memory_space_constraint(x, pltpu.HBM)

    gradient, hessian, step = pl.pallas_call(
        kernel,
        out_shape=(
            jax.ShapeDtypeStruct((cells, width), f32),
            jax.ShapeDtypeStruct((cells, width), f32),
            jax.ShapeDtypeStruct((1, 1), f32),
        ),
        in_specs=[any_space] * 7,
        out_specs=(any_space, any_space, pl.BlockSpec(memory_space=pltpu.VMEM)),
        scratch_shapes=[
            pltpu.VMEM((HALVES, cells, LANES), f32),
            pltpu.VMEM((NT * cells, width), jnp.bfloat16),
            pltpu.VMEM((HALVES, NT * cells, LANES), f32),
            pltpu.VMEM((NT, ROWS, HALVES, MEMBERS, LANES), f32),
            pltpu.VMEM((2, HALVES, ROWS, LANES), f32),
            pltpu.VMEM((HALVES, ROWS, LANES), jnp.int32),
            pltpu.VMEM((2, HALVES, NT * ROWS, LANES), f32),
            pltpu.VMEM((3, HALVES, EXT, LANES), f32),
            pltpu.VMEM((10, HALVES, EXT, LANES), f32),
            *[lines(EXT)] * 8,
            sums(NT * HALVES),
            sums(NT * HALVES),
            sums(NT * HALVES),
            sums(NT * HALVES + 1),
            pltpu.VMEM((4, NT * HALVES, SUB, LANES), f32),
            pltpu.VMEM((TILE_COUNT, 1, LANES), f32),
            pltpu.VMEM((HALVES, cells, LANES), f32),
            pltpu.VMEM((HALVES, cells, LANES), f32),
            pltpu.SemaphoreType.DMA((13,)),
            pltpu.SemaphoreType.DMA((4,)),
            pltpu.SemaphoreType.DMA((18,)),
            pltpu.SemaphoreType.DMA((18,)),
            pltpu.SemaphoreType.DMA((4, MEM_COUNT)),
            pltpu.SemaphoreType.DMA((4, MEM_COUNT)),
            pltpu.SemaphoreType.DMA,
            pltpu.SemaphoreType.DMA,
            pltpu.SemaphoreType.REGULAR((2,)),
        ],
        compiler_params=pltpu.CompilerParams(
            collective_id=0, has_side_effects=True, vmem_limit_bytes=20 << 20
        ),
    )(
        pin(control.reshape(cells, width)),
        pin(perturbations.reshape(NT * cells, width)),
        pin(innovation.reshape(NT * ROWS, width)),
        pin(obs_weight.reshape(NT * ROWS, width)),
        pin(diffusion),
        pin(advection),
        pin(upwind),
    )
    gradient, hessian = pl.pallas_call(
        hand_over,
        out_shape=(jax.ShapeDtypeStruct((cells, width), f32),) * 2,
        in_specs=[any_space] * 2,
        out_specs=(any_space, any_space),
        scratch_shapes=[pltpu.SemaphoreType.DMA((2,))], compiler_params=pltpu.CompilerParams(vmem_limit_bytes=1 << 20),
    )(gradient, hessian)
    return (
        gradient.reshape(control.shape),
        hessian.reshape(control.shape),
        step.reshape(()),
    )


def solution(mesh):
    return jax.shard_map(
        shards,
        mesh=mesh,
        in_specs=(
            P(None, "mem", "tile", None),
            P("mem", "tile", None),
            P(None, "tile", None),
            P(None, "tile", None),
            P("tile", None),
            P("tile", None),
            P("tile", None),
        ),
        out_specs=(P("mem", "tile", None), P("mem", "tile", None), P()),
        check_vma=False,
    )
```
